128 devices in a mesh: rows: 128 (over y, x, z, core).
Axes of the slice: x: 4, y: 4, z: 4, core: 2. Of those that a mesh axis runs over, the one named last changes fastest.
Arguments:
- left: bfloat16 [524288, 512], P('rows'), may hold values from -24 to 24
- right: bfloat16 [524288, 512], P('rows'), may hold values from -6 to 6
- tiles: bfloat16 [2, 64, 128, 128], replicated, may hold values from -0.1875 to 0.1875
- source_blocks: int32 [2, 4096, 16], P(None, 'rows'), may hold values from 0 to 287, as said below
- tile_index: int32 [2, 4096, 16], P(None, 'rows'), may hold values from -1 to 63
- send_blocks: int32 [16384, 2], P('rows'), may hold values from -1 to 31, as said below
Outputs:
- moments: float32 [2, 512, 512], P(None, 'rows')
The draws below stay inside these ranges and needn't reach their ends.
Inputs may be any that keep to these rules, and one draw needn't show every extreme that they name: `source_blocks`: every slot with v >= 32 names a slot of send_blocks that is not -1. Empty slots (tile -1) name an own block. Each provided block is named by some slot of the receiving device. Some device receives 2 blocks from every device, and some device has all of its slots filled. `send_blocks`: slot 0 is never -1; the two blocks that one device provides to another are different.
All inputs are finite; a program needn't handle non-finite values.
Results may differ from the reference program's by a relative error of at most 0.0029.
Values may be sent and summed in bfloat16 or wider, within the bound.
A program may use at most 192 MiB of HBM per device.

```python
import math
import jax
import jax.numpy as jnp
from jax import lax

ROW_BLK = 128
VEC = 512
BLK_DEV = 32
KSLOT = 16
TILES = 64
CAP = 2
ROWS = 524288
N_ROWS = 128


def joint_plan(key):
    subkeys = [jax.random.fold_in(key, 1000 + number) for number in range(12)]
    hub_device = jax.random.randint(subkeys[0], (), 0, N_ROWS)
    counts = 1 + jax.random.randint(subkeys[1], (N_ROWS, N_ROWS), 0, 2)
    receiver = jnp.arange(N_ROWS)[None, :]
    counts = jnp.where(receiver == hub_device, 2, counts)
    first_block = jax.random.randint(subkeys[2], (N_ROWS, N_ROWS), 0, BLK_DEV)
    second = (first_block + 1 + jax.random.randint(subkeys[3], (N_ROWS, N_ROWS), 0, BLK_DEV - 1)) % BLK_DEV
    send_table = jnp.stack([first_block, jnp.where(counts == 2, second, -1)], axis=-1).reshape(N_ROWS * N_ROWS, CAP)
    total_slots = 2 * BLK_DEV * KSLOT

    def one_order(subkey):
        return jax.random.permutation(subkey, total_slots)
    orders = jax.vmap(one_order)(jax.random.split(subkeys[4], N_ROWS))
    inverse = jnp.argsort(orders, axis=1, stable=True)
    position = jnp.broadcast_to(jnp.arange(total_slots)[None, :], (N_ROWS, total_slots))
    pair_peer = jnp.minimum(position // CAP, N_ROWS - 1)
    pair_slot = position % CAP
    pair_open = pair_slot < jnp.take_along_axis(counts.T, pair_peer, axis=1)
    forced = (position < N_ROWS * CAP) & pair_open
    fill_level = 1 + jax.random.randint(subkeys[5], (N_ROWS,), 0, 8)
    busy_device = jax.random.randint(subkeys[6], (), 0, N_ROWS)
    fill_level = jnp.where(jnp.arange(N_ROWS) == busy_device, 8, fill_level)
    kept_slot = jax.random.randint(subkeys[7], (N_ROWS, total_slots), 0, 8) < fill_level[:, None]
    far_slot = jax.random.randint(subkeys[8], (N_ROWS, total_slots), 0, 2) == 1
    far_peer = jax.random.randint(subkeys[9], (N_ROWS, total_slots), 0, N_ROWS)
    near_block = jax.random.randint(subkeys[10], (N_ROWS, total_slots), 0, BLK_DEV)
    values = jnp.where(forced, BLK_DEV + position, jnp.where(far_slot & kept_slot, BLK_DEV + far_peer * CAP, near_block))
    active = forced | kept_slot
    chosen_tiles = jnp.where(active, jax.random.randint(subkeys[11], (N_ROWS, total_slots), 0, TILES), -1)
    values = jnp.take_along_axis(values, inverse, axis=1)
    chosen_tiles = jnp.take_along_axis(chosen_tiles, inverse, axis=1)
    values = values.reshape(N_ROWS, 2, BLK_DEV, KSLOT).transpose(1, 0, 2, 3).reshape(2, N_ROWS * BLK_DEV, KSLOT)
    chosen_tiles = chosen_tiles.reshape(N_ROWS, 2, BLK_DEV, KSLOT).transpose(1, 0, 2, 3).reshape(2, N_ROWS * BLK_DEV, KSLOT)
    return (values.astype(jnp.int32), chosen_tiles.astype(jnp.int32), send_table.astype(jnp.int32))


def draw_source_blocks(key, part):
    return joint_plan(key)[0]


def draw_tile_index(key, part):
    return joint_plan(key)[1]


def draw_send_blocks(key, part):
    return joint_plan(key)[2]


def raised(result, own_key, source, target, shards_of, factor):
    owner, partner = [(jnp.arange(result.shape[dim]) // (result.shape[dim] // shards_of)).reshape([-1 if axis == dim else 1 for axis in range(result.ndim)]) for dim in (source, target)]
    chosen = jax.random.permutation(own_key, shards_of)[partner]
    strong = (owner == chosen) | (owner == (partner + shards_of // 2) % shards_of)
    return jnp.where(strong, factor * result, result)


def block_scale(own_key, extent, cuts, smallest, largest):
    loudness, own = 1.0, jax.random.fold_in(own_key, 6)
    for dim, blocks in cuts:
        draws = jnp.exp(jax.random.uniform(jax.random.fold_in(own, dim), (blocks,), jnp.float32, smallest / len(cuts), largest / len(cuts)))
        loudness = loudness * jnp.repeat(draws, extent[dim] // blocks).reshape([-1 if axis == dim else 1 for axis in range(len(extent))])
    return loudness


def normal_values(own_key, extent, deviation, most, cuts=(), kind=jnp.bfloat16):
    level = block_scale(own_key, extent, cuts, -0.22, 0.18) if cuts else 1.0
    drawn = jax.random.normal(own_key, extent, jnp.float32) * deviation * level
    return jnp.minimum(jnp.maximum(drawn, -most), most).astype(kind)


def noise_with(own_key, extent, spread, limit, cuts, heavy, held_as=jnp.bfloat16):
    entries = spread * jax.random.normal(own_key, extent, jnp.float32)
    if cuts:
        entries = entries * block_scale(own_key, extent, cuts, -0.22, 0.18)
    return jnp.clip(raised(entries, jax.random.fold_in(own_key, 3), *heavy), -limit, limit).astype(held_as)


def setup_inputs(seed: int = 0) -> dict:
    streams_of = jax.random.split(jax.random.key(seed), 7)
    left = noise_with(streams_of[0], (ROWS, VEC), 1.0, 24.0, ((0, 128),), (0, 1, 128, 5.5))
    right = normal_values(streams_of[1], (ROWS, VEC), 1.0, 6.0, ((0, 128),))
    tiles = normal_values(streams_of[2], (2, TILES, ROW_BLK, ROW_BLK), (ROW_BLK * KSLOT // 2) ** -0.5, 0.1875)
    source_blocks = draw_source_blocks(jax.random.fold_in(streams_of[6], 71), 0)
    tile_index = draw_tile_index(jax.random.fold_in(streams_of[6], 71), 0)
    send_blocks = draw_send_blocks(jax.random.fold_in(streams_of[6], 71), 0)
    return {"left": left, "right": right, "tiles": tiles, "source_blocks": source_blocks, "tile_index": tile_index, "send_blocks": send_blocks}


def resolve(values, send_blocks):
    owner_device = (jnp.arange(values.shape[0], dtype=jnp.int32) // BLK_DEV)[:, None]
    remote = values >= BLK_DEV
    offset = jnp.maximum(values - BLK_DEV, 0)
    peer_device = offset // CAP
    peer_slot = offset % CAP
    provided = send_blocks[peer_device * N_ROWS + owner_device, peer_slot]
    return jnp.where(remote, peer_device * BLK_DEV + provided, owner_device * BLK_DEV + values).astype(jnp.int32)

def reference(left, right, tiles, source_blocks, tile_index, send_blocks):
    total_blocks = BLK_DEV * N_ROWS
    blocks = right.reshape(total_blocks, ROW_BLK, VEC)
    norm_scale = 1.0 / math.sqrt(total_blocks * ROW_BLK)
    group_size = 8
    results = []
    for direction in range(2):
        global_source = resolve(source_blocks[direction], send_blocks)
        tile_table = tiles[direction]

        def one_group(operands):
            group_sources, group_tiles = operands
            live = (group_tiles >= 0)[..., None, None]
            chosen = jnp.where(live, tile_table[jnp.maximum(group_tiles, 0)], jnp.zeros((), jnp.bfloat16))
            picked = blocks[group_sources]
            summed = jnp.einsum('bkij,bkjn->bin', chosen.astype(jnp.float32), picked.astype(jnp.float32))
            return summed.astype(jnp.bfloat16)
        current = lax.map(one_group, (global_source.reshape(-1, group_size, KSLOT), tile_index[direction].reshape(-1, group_size, KSLOT)))
        current = current.reshape(total_blocks * ROW_BLK, VEC)
        gram = lax.dot_general(left, current, (((0,), (0,)), ((), ())), preferred_element_type=jnp.float32)
        results.append(gram * norm_scale)
    return jnp.stack(results)
```

```python
import functools
import math

import jax
import jax.numpy as jnp
from jax import lax
from jax.experimental import pallas as pl
from jax.experimental.pallas import tpu as pltpu
from jax.sharding import PartitionSpec as P

MESH = pl.DeviceIdType.MESH
BF16, F32, I32 = jnp.bfloat16, jnp.float32, jnp.int32

STRIDE = (2, 8, 32)


def coord(me, axis):
    return (me // STRIDE[axis]) % 4


def right_mate(me, axis):
    return me + STRIDE[axis] * (1 - 2 * (coord(me, axis) % 2))


def left_mate(me, axis):
    return me + STRIDE[axis] * (3 - 2 * coord(me, axis))


def other_core(me):
    return me + 1 - 2 * (me % 2)


def cut(rows, unit):
    third = rows // unit // 3
    sizes = [rows - 2 * third * unit, third * unit, third * unit]
    starts = [0, sizes[0], sizes[0] + sizes[1]]
    return list(zip(starts, sizes))


class Cube:
    def __init__(self, own, held, parts, mates, send, recv):
        self.own, self.held, self.parts, self.mates = own, held, parts, mates
        self.send, self.recv = send, recv

    def part(self, unit, p):
        start, size = self.parts[p]
        ref = self.own if unit == 0 else self.held.at[unit]
        return ref.at[pl.ds(start, size)]

    def hop(self, p, unit, axis):
        start, size = self.parts[p]
        into = unit + (1 << axis)
        at = p * 8 + into
        return pltpu.make_async_remote_copy(
            src_ref=self.part(unit, p),
            dst_ref=self.held.at[into].at[pl.ds(start, size)],
            send_sem=self.send.at[at],
            recv_sem=self.recv.at[at],
            device_id=(self.mates[axis],),
            device_id_type=MESH,
        )

    def order(self, p):
        return [(p + n) % 3 for n in range(3)]

    def phases(self):
        result = [[] for _ in range(7)]
        for p in range(len(self.parts)):
            a, b, c = self.order(p)
            ua, ub = 1 << a, 1 << b
            for n, (unit, axis) in enumerate(
                [(0, a), (0, b), (ua, b), (0, c), (ua, c), (ub, c), (ua + ub, c)]
            ):
                result[n].append((p, unit, axis))
        return result

    def start_own(self, axis_place):
        for p in range(len(self.parts)):
            self.hop(p, 0, self.order(p)[axis_place]).start()

    def forward(self, p, unit, axis):
        got = unit + (1 << axis)
        order = self.order(p)
        for later in order[order.index(axis) + 1 :]:
            self.hop(p, got, later).start()

    def drain(self):
        for phase in self.phases():
            for hop in phase:
                self.hop(*hop).wait_send()


def gather_kernel(
    blocks, per_dir, slots,
    source_ref, tile_ref, left_ref, right_ref, block_ref, tiles_ref, need_ref, sent_ref,
    rights, lefts, needs, sents, total_ref,
    own_right, own_left, own_turned, tile_table, current, total,
    local_sem, r_send, r_recv, l_send, l_recv, n_send, n_recv, s_send, s_recv, c_send, c_recv, d_send, d_recv,
):
    me = lax.axis_index("rows")
    right_mates = [right_mate(me, axis) for axis in range(3)]
    left_mates = [left_mate(me, axis) for axis in range(3)]
    twin = other_core(me)

    barrier = pltpu.get_barrier_semaphore()
    for mate in right_mates + left_mates + [twin]:
        pl.semaphore_signal(barrier, inc=1, device_id=(mate,), device_id_type=MESH)

    left_in = pltpu.make_async_copy(left_ref, own_left, local_sem.at[0])
    left_in.start()
    right_in = pltpu.make_async_copy(block_ref, own_right, local_sem.at[1])
    right_in.start()
    tiles_in = pltpu.make_async_copy(tiles_ref, tile_table.at[pl.ds(0, tiles_ref.shape[0])], local_sem.at[2])
    tiles_in.start()
    pl.semaphore_wait(barrier, 7)

    rows = right_ref.shape[0]
    turned_rows = own_turned.shape[0]
    right_cube = Cube(right_ref, rights.at[0], cut(rows, 16), right_mates, r_send, r_recv)
    left_cube = Cube(own_turned, lefts, cut(turned_rows, 16), left_mates, l_send, l_recv)
    need_cube = Cube(need_ref, needs, [(0, need_ref.shape[0])], left_mates, n_send, n_recv)
    sent_cube = Cube(sent_ref, sents.at[0], [(0, sent_ref.shape[0])], right_mates, s_send, s_recv)

    def across(p, unit):
        start, size = right_cube.parts[p]
        at = p * 8 + unit
        return pltpu.make_async_remote_copy(
            src_ref=right_cube.part(unit, p),
            dst_ref=rights.at[1].at[unit].at[pl.ds(start, size)],
            send_sem=c_send.at[at], recv_sem=c_recv.at[at], device_id=(twin,), device_id_type=MESH,
        )

    def across_sent(unit):
        return pltpu.make_async_remote_copy(
            src_ref=sent_cube.part(unit, 0), dst_ref=sents.at[1].at[unit],
            send_sem=d_send.at[unit], recv_sem=d_recv.at[unit], device_id=(twin,), device_id_type=MESH,
        )

    for place in range(3):
        right_cube.start_own(place)
    for place in range(3):
        need_cube.start_own(place)
        sent_cube.start_own(place)
    across_sent(0).start()
    for p in range(3):
        across(p, 0).start()

    left_in.wait()
    block_rows = left_ref.shape[0] // blocks
    vectors = left_ref.shape[1]

    def turn(b, _):
        at = pl.multiple_of(b * block_rows, block_rows)
        to = pl.multiple_of(b * vectors, vectors)
        own_turned[pl.ds(to, vectors), :] = own_left[pl.ds(at, block_rows), :].T
        return 0

    lax.fori_loop(0, blocks, turn, 0)
    for place in range(3):
        left_cube.start_own(place)
    left_out = pltpu.make_async_copy(own_turned, lefts.at[0], local_sem.at[3])
    left_out.start()
    right_out = pltpu.make_async_copy(right_ref, rights.at[0].at[0], local_sem.at[4])
    right_out.start()
    need_out = pltpu.make_async_copy(need_ref, needs.at[0], local_sem.at[5])
    need_out.start()
    sent_out = pltpu.make_async_copy(sent_ref, sents.at[0].at[0], local_sem.at[6])
    sent_out.start()

    tiles_in.wait()
    right_in.wait()
    zero_tile = tiles_ref.shape[0]
    tile_table[zero_tile] = jnp.zeros(tile_table.shape[1:], BF16)
    total[...] = jnp.zeros_like(total)
    group = 8
    groups = blocks // group

    def own_group(n, _):
        d = n // groups
        first = (n % groups) * group

        def row(e, _):
            b = first + e
            summed = jnp.zeros((block_rows, vectors), F32)
            for k0 in range(0, slots, 4):
                chosen, picked = [], []
                for k in range(k0, k0 + 4):
                    chosen.append(tile_table[tile_ref[d, b, k]])
                    picked.append(own_right[source_ref[d, b, k]])
                summed = summed + jnp.dot(
                    jnp.concatenate(chosen, axis=1), jnp.concatenate(picked, axis=0), preferred_element_type=F32
                )
            current[pl.ds(pl.multiple_of(e * block_rows, block_rows), block_rows), :] = summed.astype(BF16)
            return 0

        lax.fori_loop(0, group, row, 0)
        turned = jnp.concatenate(
            [own_turned[pl.ds(pl.multiple_of((first + e) * vectors, vectors), vectors), :] for e in range(group)], axis=1
        )
        total[d] = total[d] + jnp.dot(turned, current[...], preferred_element_type=F32)
        return 0

    def compute(lo, hi):
        lax.fori_loop(lo, hi, own_group, 0)

    plan = {0: (0, 3), 1: (3, 5), 2: (5, 8)}
    phases = list(zip(right_cube.phases(), left_cube.phases()))
    small = list(zip(need_cube.phases(), sent_cube.phases()))
    for n in range(7):
        if n in plan:
            compute(*plan[n])
        if n == 3:
            total_out = pltpu.make_async_copy(total, total_ref, local_sem.at[7])
            total_out.start()
        for hop in small[n][0]:
            need_cube.hop(*hop).wait_recv()
            need_cube.forward(*hop)
        for hop in small[n][1]:
            sent_cube.hop(*hop).wait_recv()
            sent_cube.forward(*hop)
            across_sent(hop[1] + (1 << hop[2])).start()
        for hop, lhop in zip(*phases[n]):
            right_cube.hop(*hop).wait_recv()
            right_cube.forward(*hop)
            across(hop[0], hop[1] + (1 << hop[2])).start()
            left_cube.hop(*lhop).wait_recv()
            left_cube.forward(*lhop)
    for cube in (right_cube, left_cube, need_cube, sent_cube):
        cube.drain()
    for unit in range(8):
        across_sent(unit).wait()
        for p in range(3):
            across(p, unit).wait()
    for copy in (left_out, right_out, need_out, sent_out, total_out):
        copy.wait()


def gather(left, right, tiles, source_blocks, tile_index, need, sent):
    rows, vectors = right.shape
    block_rows = tiles.shape[-1]
    blocks = rows // block_rows
    table = tiles.reshape(-1, block_rows, block_rows)
    offset = jnp.arange(2, dtype=I32)[:, None, None] * tiles.shape[1]
    own = jnp.logical_and(tile_index >= 0, source_blocks < blocks)
    tile_index = jnp.where(own, tile_index + offset, table.shape[0])
    source_blocks = jnp.where(own, source_blocks, 0)
    any_spec = pl.BlockSpec(memory_space=pl.ANY)
    smem = pl.BlockSpec(memory_space=pltpu.SMEM)
    dma = pltpu.SemaphoreType.DMA
    return pl.pallas_call(
        functools.partial(gather_kernel, blocks, source_blocks.shape[1], source_blocks.shape[2]),
        out_shape=(
            jax.ShapeDtypeStruct((2, 8, rows, vectors), BF16),
            jax.ShapeDtypeStruct((8, blocks * vectors, block_rows), BF16),
            jax.ShapeDtypeStruct((8,) + need.shape, I32),
            jax.ShapeDtypeStruct((2, 8) + sent.shape, I32),
            jax.ShapeDtypeStruct((2, vectors, vectors), F32),
        ),
        in_specs=[smem, smem] + [any_spec] * 6,
        out_specs=(any_spec,) * 5,
        scratch_shapes=[
            pltpu.VMEM((blocks, block_rows, vectors), BF16),
            pltpu.VMEM((rows, vectors), BF16),
            pltpu.VMEM((blocks * vectors, block_rows), BF16),
            pltpu.VMEM((table.shape[0] + 1, block_rows, block_rows), BF16),
            pltpu.VMEM((8 * block_rows, vectors), BF16),
            pltpu.VMEM((2, vectors, vectors), F32),
            dma((8,)),
            dma((24,)), dma((24,)), dma((24,)), dma((24,)),
            dma((8,)), dma((8,)), dma((8,)), dma((8,)),
            dma((24,)), dma((24,)), dma((8,)), dma((8,)),
        ],
        compiler_params=pltpu.CompilerParams(
            collective_id=0, has_side_effects=True, vmem_limit_bytes=56 << 20
        ),
        name="gather",
    )(source_blocks, tile_index, left, right, right.reshape(blocks, block_rows, vectors), table, need, sent)


GROUP = 8
DEPTH = 3


def far_kernel(
    blocks, slots, tiles_dir,
    rights, lefts, needs, sents, tiles_ref, total_in, total_ref,
    need_s, sent_s, terms, tile_table, right_buf, left_buf, current, total, sem, rsem, lsem,
):
    me = lax.axis_index("rows")
    block_rows, vectors = right_buf.shape[-2] // GROUP, right_buf.shape[-1]
    copies = [pltpu.make_async_copy(tiles_ref, tile_table.at[pl.ds(0, tiles_ref.shape[0])], sem.at[0])]
    copies.append(pltpu.make_async_copy(total_in, total, sem.at[1]))
    for j in range(8):
        copies.append(pltpu.make_async_copy(needs.at[j, j], need_s.at[j], sem.at[2 + j]))
    for c in range(2):
        for i in range(8):
            copies.append(pltpu.make_async_copy(sents.at[c, i], sent_s.at[c * 8 + i], sem.at[10 + c * 8 + i]))
    for copy in copies:
        copy.start()
    for copy in copies[2:]:
        copy.wait()

    zero_tile = 2 * tiles_dir

    def pack(row, holder, code):
        code = jnp.maximum(code - 1, 0)
        tile = code % tiles_dir
        slot = code // tiles_dir
        at = (slot // 2, holder * 2 + slot % 2)
        block = sent_s[at[0], at[1] // 128, at[1] % 128]
        return ((row * 16 + slot // 2) * blocks + jnp.maximum(block, 0)) * tiles_dir + tile

    def list_dir(d, start):
        def unit(j, pos):
            z, x, y = coord(me, 0), coord(me, 1), coord(me, 2)
            z = jnp.where(j % 2 == 1, 3 - z, z)
            x = jnp.where((j // 2) % 2 == 1, 3 - x, x)
            y = jnp.where(j // 4 == 1, 3 - y, y)
            holder = y * STRIDE[2] + x * STRIDE[1] + z * STRIDE[0] + me % 2

            def one_row(b, pos):
                at = (d * blocks + b) * slots
                line, lane = at // 128, at % 128
                row = j * blocks + b

                def more(state):
                    k, pos = state
                    terms[pos] = pack(row, holder, need_s[j, line, lane + k])
                    return k + 1, pos + 1

                def going(state):
                    k, _ = state
                    return jnp.logical_and(k < slots, need_s[j, line, lane + jnp.minimum(k, slots - 1)] > 0)

                return lax.while_loop(going, more, (jnp.int32(0), pos))[1]

            return lax.fori_loop(0, blocks, one_row, pos)

        pos = lax.fori_loop(0, 8, unit, start)
        end = (pos + GROUP - 1) // GROUP * GROUP

        def fill(n, _):
            terms[n] = -1
            return 0

        lax.fori_loop(pos, end, fill, 0)
        return end

    half = list_dir(0, jnp.int32(0))
    end = list_dir(1, half)
    count = end // GROUP
    half = half // GROUP

    def fetch(g, e):
        word = jnp.maximum(terms[g * GROUP + e], 0)
        slot = g % DEPTH
        block = (word // tiles_dir) % blocks
        provider = (word // (tiles_dir * blocks)) % 16
        row = word // (tiles_dir * blocks * 16)
        right = pltpu.make_async_copy(
            rights.at[provider // 8, provider % 8, pl.ds(pl.multiple_of(block * block_rows, block_rows), block_rows)],
            right_buf.at[slot, pl.ds(e * block_rows, block_rows)],
            rsem.at[slot, e],
        )
        left = pltpu.make_async_copy(
            lefts.at[row // blocks, pl.ds(pl.multiple_of((row % blocks) * vectors, vectors), vectors)],
            left_buf.at[slot, e],
            lsem.at[slot, e],
        )
        return right, left

    def start(g):
        for e in range(GROUP):
            for copy in fetch(g, e):
                copy.start()

    for g in range(DEPTH - 1):
        @pl.when(g < count)
        def _():
            start(g)

    for copy in copies[:2]:
        copy.wait()
    tile_table[zero_tile] = jnp.zeros(tile_table.shape[1:], BF16)

    def step(g, _):
        @pl.when(g + DEPTH - 1 < count)
        def _():
            start(g + DEPTH - 1)

        d = jnp.where(g >= half, 1, 0)
        slot = g % DEPTH
        for e in range(GROUP):
            right, left = fetch(g, e)
            right.wait()
            left.wait()
        for e in range(GROUP):
            word = terms[g * GROUP + e]
            tile = jnp.where(word >= 0, d * tiles_dir + jnp.maximum(word, 0) % tiles_dir, zero_tile)
            current[pl.ds(e * block_rows, block_rows), :] = jnp.dot(
                tile_table[tile], right_buf[slot, pl.ds(e * block_rows, block_rows), :], preferred_element_type=F32
            ).astype(BF16)
        turned = jnp.concatenate([left_buf[slot, e] for e in range(GROUP)], axis=1)
        total[d] = total[d] + jnp.dot(turned, current[...], preferred_element_type=F32)
        return 0

    lax.fori_loop(0, count, step, 0)
    out = pltpu.make_async_copy(total, total_ref, sem.at[0])
    out.start()
    out.wait()


def far(blocks, slots, rights, lefts, needs, sents, tiles, total):
    rows, vectors = rights.shape[2:]
    block_rows = tiles.shape[-1]
    tiles_dir = tiles.shape[1]
    table = tiles.reshape(-1, block_rows, block_rows)
    any_spec = pl.BlockSpec(memory_space=pl.ANY)
    dma = pltpu.SemaphoreType.DMA
    return pl.pallas_call(
        functools.partial(far_kernel, blocks, slots, tiles_dir),
        out_shape=jax.ShapeDtypeStruct(total.shape, F32),
        in_specs=[any_spec] * 6,
        out_specs=any_spec,
        scratch_shapes=[
            pltpu.SMEM((8,) + needs.shape[2:], I32),
            pltpu.SMEM((16,) + sents.shape[2:], I32),
            pltpu.SMEM((8 * 2 * blocks * slots + 2 * GROUP,), I32),
            pltpu.VMEM((table.shape[0] + 1, block_rows, block_rows), BF16),
            pltpu.VMEM((DEPTH, GROUP * block_rows, vectors), BF16),
            pltpu.VMEM((DEPTH, GROUP, vectors, block_rows), BF16),
            pltpu.VMEM((GROUP * block_rows, vectors), BF16),
            pltpu.VMEM(total.shape, F32),
            dma((26,)), dma((DEPTH, GROUP)), dma((DEPTH, GROUP)),
        ],
        compiler_params=pltpu.CompilerParams(vmem_limit_bytes=56 << 20),
        name="far",
    )(rights, lefts, needs, sents, table, total)


def reduce_kernel(scale, total_ref, out_ref, half, sums, got_core, got_y, got_x, got_z, last, send, recv):
    me = lax.axis_index("rows")
    core = me % 2
    twin = other_core(me)

    def at(axis, n):
        c = coord(me, axis)
        return me + STRIDE[axis] * ((c + n) % 4 - c)

    peers = [twin] + [at(axis, n) for axis in range(3) for n in range(1, 4)]
    barrier = pltpu.get_barrier_semaphore()
    for peer in peers:
        pl.semaphore_signal(barrier, inc=1, device_id=(peer,), device_id_type=MESH)
    pl.semaphore_wait(barrier, len(peers))

    def copy(n, src, dst, peer):
        return pltpu.make_async_remote_copy(
            src_ref=src, dst_ref=dst, send_sem=send.at[n], recv_sem=recv.at[n], device_id=(peer,), device_id_type=MESH
        )

    swap = copy(0, total_ref.at[1 - core], got_core, twin)
    swap.start()
    swap.wait()
    half[...] = (total_ref[core] + got_core[...]) * scale

    source, size = half, half.shape[0]
    for stage, (axis, got) in enumerate(((2, got_y), (1, got_x), (0, got_z))):
        part = size // 4
        c = coord(me, axis)
        copies = []
        for n in (2, 1, 3):
            theirs = pl.multiple_of(((c + n) % 4) * part, 8)
            copies.append(copy(1 + stage * 3 + n - 1, source.at[pl.ds(theirs, part)], got.at[n - 1], at(axis, n)))
            copies[-1].start()
        for one in copies:
            one.wait()
        mine = pl.multiple_of(c * part, 8)
        into = sums.at[stage]
        into[pl.ds(0, part), :] = source[pl.ds(mine, part), :] + got[0] + got[1] + got[2]
        source, size = into, part
    give = copy(10, source.at[pl.ds(0, size)], last, twin)
    give.start()
    give.wait()
    keep = size // 2
    mine, other = source[pl.ds(0, size), :], last[...]
    first = jnp.where(core == 0, mine[:keep], other[keep:])
    second = jnp.where(core == 0, other[:keep], mine[keep:])
    out_ref[0] = first
    out_ref[1] = second


def reduce(total, scale, devices):
    _, vectors, width = total.shape
    vm = pl.BlockSpec(memory_space=pltpu.VMEM)
    return pl.pallas_call(
        functools.partial(reduce_kernel, scale),
        out_shape=jax.ShapeDtypeStruct((2, vectors // devices, width), F32),
        in_specs=[vm],
        out_specs=vm,
        scratch_shapes=[
            pltpu.VMEM((vectors, width), F32),
            pltpu.VMEM((3, vectors // 4, width), F32),
            pltpu.VMEM((vectors, width), F32),
            pltpu.VMEM((3, vectors // 4, width), F32),
            pltpu.VMEM((3, vectors // 16, width), F32),
            pltpu.VMEM((3, vectors // 64, width), F32),
            pltpu.VMEM((vectors // 64, width), F32),
            pltpu.SemaphoreType.DMA((11,)),
            pltpu.SemaphoreType.DMA((11,)),
        ],
        compiler_params=pltpu.CompilerParams(
            collective_id=1, has_side_effects=True, vmem_limit_bytes=32 << 20
        ),
        name="reduce",
    )(total)


def needs_of(source_blocks, tile_index, blocks, tiles_dir):
    me = lax.axis_index("rows")
    far_slot = jnp.maximum(source_blocks - blocks, 0)
    peer, copy = far_slot // 2, far_slot % 2
    differ = peer ^ me
    low = [(differ // STRIDE[axis]) % 2 for axis in range(3)]
    high = [(differ // (2 * STRIDE[axis])) % 2 for axis in range(3)]
    left_unit = high[0] + 2 * high[1] + 4 * high[2]
    right_unit = (low[0] ^ high[0]) + 2 * (low[1] ^ high[1]) + 4 * (low[2] ^ high[2])
    provider = (differ % 2) * 8 + right_unit
    code = (provider * 2 + copy) * tiles_dir + jnp.maximum(tile_index, 0) + 1
    live = jnp.logical_and(tile_index >= 0, source_blocks >= blocks)
    unit = jnp.where(live, left_unit, -1).reshape(-1, source_blocks.shape[-1])
    code = code.reshape(unit.shape)
    mine = unit[None] == jnp.arange(8, dtype=I32)[:, None, None]
    slots = unit.shape[-1]
    earlier = jnp.arange(slots)[:, None] < jnp.arange(slots)[None, :]
    place = jnp.sum(jnp.where(earlier[None, None], mine[..., :, None].astype(I32), 0), axis=2)
    hit = jnp.logical_and(mine[..., None, :], place[..., None, :] == jnp.arange(slots, dtype=I32)[:, None])
    packed = jnp.sum(jnp.where(hit, code[None, :, None, :], 0), axis=-1)
    return packed.reshape(8, -1, 128)


def body(left, right, tiles, source_blocks, tile_index, send_blocks):
    block_rows = tiles.shape[-1]
    rows, _ = right.shape
    blocks = rows // block_rows
    devices = lax.axis_size("rows")
    scale = 1.0 / math.sqrt(rows * devices)
    need = needs_of(source_blocks, tile_index, blocks, tiles.shape[1])
    sent = send_blocks.reshape(-1, 128)
    rights, lefts, needs, sents, total = gather(left, right, tiles, source_blocks, tile_index, need, sent)
    total = far(blocks, source_blocks.shape[2], rights, lefts, needs, sents, tiles, total)
    return reduce(total, scale, devices)


def solution(mesh):
    placed = (
        P("rows", None),
        P("rows", None),
        P(),
        P(None, "rows", None),
        P(None, "rows", None),
        P("rows", None),
    )
    return jax.shard_map(
        body, mesh=mesh, in_specs=placed, out_specs=P(None, "rows", None), check_vma=False
    )
```

```python
import functools
import math

import jax
import jax.numpy as jnp
from jax import lax
from jax.experimental import pallas as pl
from jax.experimental.pallas import tpu as pltpu
from jax.sharding import PartitionSpec as P

MESH = pl.DeviceIdType.MESH
BF16, F32, I32 = jnp.bfloat16, jnp.float32, jnp.int32

STRIDE = (2, 8, 32)


def coord(me, axis):
    return (me // STRIDE[axis]) % 4


def right_mate(me, axis):
    return me + STRIDE[axis] * (1 - 2 * (coord(me, axis) % 2))


def left_mate(me, axis):
    return me + STRIDE[axis] * (3 - 2 * coord(me, axis))


def other_core(me):
    return me + 1 - 2 * (me % 2)


def cut(rows, unit):
    third = rows // unit // 3
    sizes = [rows - 2 * third * unit, third * unit, third * unit]
    starts = [0, sizes[0], sizes[0] + sizes[1]]
    return list(zip(starts, sizes))


class Cube:
    def __init__(self, own, held, parts, mates, send, recv):
        self.own, self.held, self.parts, self.mates = own, held, parts, mates
        self.send, self.recv = send, recv

    def part(self, unit, p):
        start, size = self.parts[p]
        ref = self.own if unit == 0 else self.held.at[unit]
        return ref.at[pl.ds(start, size)]

    def hop(self, p, unit, axis):
        start, size = self.parts[p]
        into = unit + (1 << axis)
        at = p * 8 + into
        return pltpu.make_async_remote_copy(
            src_ref=self.part(unit, p),
            dst_ref=self.held.at[into].at[pl.ds(start, size)],
            send_sem=self.send.at[at],
            recv_sem=self.recv.at[at],
            device_id=(self.mates[axis],),
            device_id_type=MESH,
        )

    def order(self, p):
        return [(p + n) % 3 for n in range(3)]

    def phases(self):
        result = [[] for _ in range(7)]
        for p in range(len(self.parts)):
            a, b, c = self.order(p)
            ua, ub = 1 << a, 1 << b
            for n, (unit, axis) in enumerate(
                [(0, a), (0, b), (ua, b), (0, c), (ua, c), (ub, c), (ua + ub, c)]
            ):
                result[n].append((p, unit, axis))
        return result

    def start_own(self, axis_place):
        for p in range(len(self.parts)):
            self.hop(p, 0, self.order(p)[axis_place]).start()

    def forward(self, p, unit, axis):
        got = unit + (1 << axis)
        order = self.order(p)
        for later in order[order.index(axis) + 1 :]:
            self.hop(p, got, later).start()

    def drain(self):
        for phase in self.phases():
            for hop in phase:
                self.hop(*hop).wait_send()


def gather_kernel(
    blocks, slots,
    source_ref, tile_ref, left_ref, right_ref, block_ref, tiles_ref, info_ref, sent_ref,
    rights, lefts, needs, sents, total_ref,
    own_right, own_left, own_turned, tile_table, current, total, info, place_of, need_ref,
    local_sem, r_send, r_recv, l_send, l_recv, n_send, n_recv, s_send, s_recv, c_send, c_recv, d_send, d_recv,
):
    me = lax.axis_index("rows")
    right_mates = [right_mate(me, axis) for axis in range(3)]
    left_mates = [left_mate(me, axis) for axis in range(3)]
    twin = other_core(me)

    info_in = pltpu.make_async_copy(info_ref, info, local_sem.at[5])
    info_in.start()
    barrier = pltpu.get_barrier_semaphore()
    for mate in right_mates + left_mates + [twin]:
        pl.semaphore_signal(barrier, inc=1, device_id=(mate,), device_id_type=MESH)

    left_in = pltpu.make_async_copy(left_ref, own_left, local_sem.at[0])
    left_in.start()
    right_in = pltpu.make_async_copy(block_ref, own_right, local_sem.at[1])
    right_in.start()
    tiles_in = pltpu.make_async_copy(tiles_ref, tile_table.at[pl.ds(0, tiles_ref.shape[0])], local_sem.at[2])
    tiles_in.start()
    pl.semaphore_wait(barrier, 7)

    rows = right_ref.shape[0]
    turned_rows = own_turned.shape[0]
    right_cube = Cube(right_ref, rights.at[0], cut(rows, 16), right_mates, r_send, r_recv)
    left_cube = Cube(own_turned, lefts, cut(turned_rows, 16), left_mates, l_send, l_recv)
    need_cube = Cube(need_ref, needs, [(0, need_ref.shape[0])], left_mates, n_send, n_recv)
    sent_cube = Cube(sent_ref, sents.at[0], [(0, sent_ref.shape[0])], right_mates, s_send, s_recv)

    def across(p, unit):
        start, size = right_cube.parts[p]
        at = p * 8 + unit
        return pltpu.make_async_remote_copy(
            src_ref=right_cube.part(unit, p),
            dst_ref=rights.at[1].at[unit].at[pl.ds(start, size)],
            send_sem=c_send.at[at], recv_sem=c_recv.at[at], device_id=(twin,), device_id_type=MESH,
        )

    def across_sent(unit):
        return pltpu.make_async_remote_copy(
            src_ref=sent_cube.part(unit, 0), dst_ref=sents.at[1].at[unit],
            send_sem=d_send.at[unit], recv_sem=d_recv.at[unit], device_id=(twin,), device_id_type=MESH,
        )

    for place in range(3):
        right_cube.start_own(place)
    for place in range(3):
        sent_cube.start_own(place)
    across_sent(0).start()
    for p in range(3):
        across(p, 0).start()

    left_in.wait()
    block_rows = left_ref.shape[0] // blocks
    vectors = left_ref.shape[1]

    def turn(b, _):
        at = pl.multiple_of(b * block_rows, block_rows)
        to = pl.multiple_of(b * vectors, vectors)
        own_turned[pl.ds(to, vectors), :] = own_left[pl.ds(at, block_rows), :].T
        return 0

    lax.fori_loop(0, blocks, turn, 0)
    for place in range(3):
        left_cube.start_own(place)
    left_out = pltpu.make_async_copy(own_turned, lefts.at[0], local_sem.at[3])
    left_out.start()
    right_out = pltpu.make_async_copy(right_ref, rights.at[0].at[0], local_sem.at[4])
    right_out.start()
    sent_out = pltpu.make_async_copy(sent_ref, sents.at[0].at[0], local_sem.at[6])
    sent_out.start()

    info_in.wait()
    many = info.shape[1]
    down = lax.broadcasted_iota(I32, (many, many), 0)
    upto = jnp.where(down <= lax.broadcasted_iota(I32, (many, many), 1), 1.0, 0.0).astype(BF16)
    eight = lax.broadcasted_iota(I32, (8, many), 0)
    for d in range(2):
        mine = jnp.broadcast_to(info[d : d + 1, :], (8, many)) == eight.astype(F32)
        ranks = jnp.dot(jnp.where(mine, 1.0, 0.0).astype(BF16), upto, preferred_element_type=F32)
        place_of[...] = jnp.where(mine, ranks, 0.0)
        words = jnp.where(eight == 0, info[2 + d : 3 + d, :], jnp.where(eight == 1, info[4 + d : 5 + d, :], 0.0))
        words = words.astype(BF16)

        def list_for(unit, _):
            hit = place_of[pl.ds(unit, 1), :] == (down + 1).astype(F32)
            found = lax.dot_general(
                words, jnp.where(hit, 1.0, 0.0).astype(BF16), (((1,), (1,)), ((), ())), preferred_element_type=F32
            )
            word = (found[0:1] * 256.0 + found[1:2]).astype(I32)
            for line in range(many // 128):
                need_ref[unit, pl.ds(d * (many // 128) + line, 1), :] = word[:, line * 128 : line * 128 + 128]
            return 0

        lax.fori_loop(0, 8, list_for, 0)
    for place in range(3):
        need_cube.start_own(place)
    need_out = pltpu.make_async_copy(need_ref, needs.at[0], local_sem.at[5])
    need_out.start()

    tiles_in.wait()
    right_in.wait()
    zero_tile = tiles_ref.shape[0]
    tile_table[zero_tile] = jnp.zeros(tile_table.shape[1:], BF16)
    total[...] = jnp.zeros_like(total)
    group = 8
    groups = blocks // group

    def own_group(n, _):
        d = n // groups
        first = (n % groups) * group

        def row(e, _):
            b = first + e
            summed = jnp.zeros((block_rows, vectors), F32)
            for k0 in range(0, slots, 4):
                chosen, picked = [], []
                for k in range(k0, k0 + 4):
                    chosen.append(tile_table[tile_ref[d, k, b]])
                    picked.append(own_right[source_ref[d, k, b]])
                summed = summed + jnp.dot(
                    jnp.concatenate(chosen, axis=1), jnp.concatenate(picked, axis=0), preferred_element_type=F32
                )
            current[pl.ds(pl.multiple_of(e * block_rows, block_rows), block_rows), :] = summed.astype(BF16)
            return 0

        lax.fori_loop(0, group, row, 0)
        turned = jnp.concatenate(
            [own_turned[pl.ds(pl.multiple_of((first + e) * vectors, vectors), vectors), :] for e in range(group)], axis=1
        )
        total[d] = total[d] + jnp.dot(turned, current[...], preferred_element_type=F32)
        return 0

    def compute(lo, hi):
        lax.fori_loop(lo, hi, own_group, 0)

    plan = {0: (0, 3), 1: (3, 5), 2: (5, 8)}
    phases = list(zip(right_cube.phases(), left_cube.phases()))
    small = list(zip(need_cube.phases(), sent_cube.phases()))
    for n in range(7):
        if n in plan:
            compute(*plan[n])
        if n == 3:
            total_out = pltpu.make_async_copy(total, total_ref, local_sem.at[7])
            total_out.start()
        for hop in small[n][0]:
            need_cube.hop(*hop).wait_recv()
            need_cube.forward(*hop)
        for hop in small[n][1]:
            sent_cube.hop(*hop).wait_recv()
            sent_cube.forward(*hop)
            across_sent(hop[1] + (1 << hop[2])).start()
        for hop, lhop in zip(*phases[n]):
            right_cube.hop(*hop).wait_recv()
            right_cube.forward(*hop)
            across(hop[0], hop[1] + (1 << hop[2])).start()
            left_cube.hop(*lhop).wait_recv()
            left_cube.forward(*lhop)
    for cube in (right_cube, left_cube, need_cube, sent_cube):
        cube.drain()
    for unit in range(8):
        across_sent(unit).wait()
        for p in range(3):
            across(p, unit).wait()
    for copy in (left_out, right_out, need_out, sent_out, total_out):
        copy.wait()


def gather(left, right, tiles, source_blocks, tile_index, info, sent):
    rows, vectors = right.shape
    block_rows = tiles.shape[-1]
    blocks = rows // block_rows
    table = tiles.reshape(-1, block_rows, block_rows)
    offset = jnp.arange(2, dtype=I32)[:, None, None] * tiles.shape[1]
    own = jnp.logical_and(tile_index >= 0, source_blocks < blocks)
    tile_index = jnp.where(own, tile_index + offset, table.shape[0])
    source_blocks = jnp.where(own, source_blocks, 0)
    any_spec = pl.BlockSpec(memory_space=pl.ANY)
    smem = pl.BlockSpec(memory_space=pltpu.SMEM)
    dma = pltpu.SemaphoreType.DMA
    return pl.pallas_call(
        functools.partial(gather_kernel, blocks, source_blocks.shape[1]),
        out_shape=(
            jax.ShapeDtypeStruct((2, 8, rows, vectors), BF16),
            pltpu.VMEM((8, blocks * vectors, block_rows), BF16),
            jax.ShapeDtypeStruct((8, 8) + (2 * info.shape[1] // 128, 128), I32),
            jax.ShapeDtypeStruct((2, 8) + sent.shape, I32),
            jax.ShapeDtypeStruct((2, vectors, vectors), F32),
        ),
        in_specs=[smem, smem] + [any_spec] * 6,
        out_specs=(any_spec, pl.BlockSpec(memory_space=pltpu.VMEM)) + (any_spec,) * 3,
        scratch_shapes=[
            pltpu.VMEM((blocks, block_rows, vectors), BF16),
            pltpu.VMEM((rows, vectors), BF16),
            pltpu.VMEM((blocks * vectors, block_rows), BF16),
            pltpu.VMEM((table.shape[0] + 1, block_rows, block_rows), BF16),
            pltpu.VMEM((8 * block_rows, vectors), BF16),
            pltpu.VMEM((2, vectors, vectors), F32),
            pltpu.VMEM(info.shape, F32),
            pltpu.VMEM(info.shape, F32),
            pltpu.VMEM((8, 2 * info.shape[1] // 128, 128), I32),
            dma((8,)),
            dma((24,)), dma((24,)), dma((24,)), dma((24,)),
            dma((8,)), dma((8,)), dma((8,)), dma((8,)),
            dma((24,)), dma((24,)), dma((8,)), dma((8,)),
        ],
        compiler_params=pltpu.CompilerParams(
            collective_id=0, has_side_effects=True, vmem_limit_bytes=28 << 20
        ),
        name="gather",
    )(source_blocks, tile_index, left, right, right.reshape(blocks, block_rows, vectors), table, info, sent)


GROUP = 16
DEPTH = 2


def far_kernel(
    blocks, many, tiles_dir,
    rights, lefts, needs, sents, tiles_ref, total_in, total_ref,
    need_s, sent_s, terms, tile_table, right_buf, current, total, sem, rsem,
):
    me = lax.axis_index("rows")
    block_rows, vectors = right_buf.shape[-2] // (2 * GROUP), right_buf.shape[-1]
    copies = [pltpu.make_async_copy(tiles_ref, tile_table.at[pl.ds(0, tiles_ref.shape[0])], sem.at[0])]
    copies.append(pltpu.make_async_copy(total_in, total, sem.at[1]))
    for j in range(8):
        copies.append(pltpu.make_async_copy(needs.at[j, j], need_s.at[j], sem.at[2 + j]))
    for c in range(2):
        for i in range(8):
            copies.append(pltpu.make_async_copy(sents.at[c, i], sent_s.at[c * 8 + i], sem.at[10 + c * 8 + i]))
    for copy in copies[2:] + copies[:2]:
        copy.start()
    for copy in copies[2:]:
        copy.wait()

    zero_tile = 2 * tiles_dir
    tile_bits = (tiles_dir - 1).bit_length()
    block_bits = (blocks - 1).bit_length()
    ADDR, ROW = 8, 8 + 4 + block_bits
    UNROLL = 4

    def list_dir(d, start):
        def unit(j, pos):
            z, x, y = coord(me, 0), coord(me, 1), coord(me, 2)
            z = jnp.where(j & 1 == 1, 3 - z, z)
            x = jnp.where(j & 2 == 2, 3 - x, x)
            y = jnp.where(j & 4 == 4, 3 - y, y)
            holder = y * STRIDE[2] + x * STRIDE[1] + z * STRIDE[0] + me % 2
            base = d * (many // 128)

            def word(k):
                return need_s[j, base + (k >> 7), k & 127]

            def more(state):
                k, pos, last, first = state
                for u in range(UNROLL):
                    w = word(k + u)
                    live = jnp.minimum(w, 1)
                    v = jnp.maximum(w - 1, 0)
                    slot = (v >> tile_bits) & 31
                    block = jnp.maximum(sent_s[slot >> 1, slot & 1, holder], 0)
                    b = v >> (tile_bits + 5)
                    address = ((slot >> 1) << block_bits) + block
                    term = (((j << block_bits) + b) << ROW) + (address << ADDR) + d * tiles_dir + (v & (tiles_dir - 1))
                    second = jnp.where(b == last, live, 0)
                    first = jnp.where(second == 1, first, term)
                    into = pos + 1 - second
                    terms[2 * into] = first
                    terms[2 * into + 1] = jnp.where(second == 1, term, zero_tile)
                    pos = jnp.where(live == 1, into, pos)
                    last = jnp.where(second == 1, -1, b)
                return k + UNROLL, pos, last, first

            def going(state):
                k = state[0]
                return jnp.logical_and(k < many, word(jnp.minimum(k, many - 1)) > 0)

            return lax.while_loop(going, more, (jnp.int32(0), pos, jnp.int32(-1), jnp.int32(0)))[1]

        pos = lax.fori_loop(0, 8, unit, start - 1) + 1
        for u in range(2 * GROUP):
            terms[2 * pos + u] = zero_tile
        return (pos + GROUP - 1) // GROUP * GROUP

    half = list_dir(0, jnp.int32(0))
    end = list_dir(1, half)
    count = end // GROUP
    half = half // GROUP

    def fetch(g, e):
        term = terms[g * 2 * GROUP + e]
        address = (term >> ADDR) & ((16 << block_bits) - 1)
        slot = g % DEPTH
        provider, block = address >> block_bits, address & (blocks - 1)
        return term & 255 != zero_tile, pltpu.make_async_copy(
            rights.at[provider >> 3, provider & 7, pl.ds(pl.multiple_of(block * block_rows, block_rows), block_rows)],
            right_buf.at[slot, pl.ds(e * block_rows, block_rows)],
            rsem.at[slot, e],
        )

    def start(g):
        for e in range(2 * GROUP):
            needed, copy = fetch(g, e)

            @pl.when(needed)
            def _():
                copy.start()

    right_buf[...] = jnp.zeros_like(right_buf)
    for g in range(DEPTH - 1):
        @pl.when(g < count)
        def _():
            start(g)

    for copy in copies[:2]:
        copy.wait()
    tile_table[zero_tile] = jnp.zeros(tile_table.shape[1:], BF16)

    def step(g, _):
        @pl.when(g + DEPTH - 1 < count)
        def _():
            start(g + DEPTH - 1)

        d = jnp.where(g >= half, 1, 0)
        slot = g % DEPTH
        for e in range(2 * GROUP):
            needed, copy = fetch(g, e)

            @pl.when(needed)
            def _():
                copy.wait()

        turned = []
        for e in range(GROUP):
            term, second = terms[g * 2 * GROUP + 2 * e], terms[g * 2 * GROUP + 2 * e + 1]
            current[pl.ds(e * block_rows, block_rows), :] = jnp.dot(
                jnp.concatenate([tile_table[term & 255], tile_table[second & 255]], axis=1),
                right_buf[slot, pl.ds(2 * e * block_rows, 2 * block_rows), :],
                preferred_element_type=F32,
            ).astype(BF16)
            row = term >> ROW
            turned.append(
                lefts[row >> block_bits, pl.ds(pl.multiple_of((row & (blocks - 1)) * vectors, vectors), vectors), :]
            )
        total[d] = total[d] + jnp.dot(jnp.concatenate(turned, axis=1), current[...], preferred_element_type=F32)
        return 0

    lax.fori_loop(0, count, step, 0)
    out = pltpu.make_async_copy(total, total_ref, sem.at[0])
    out.start()
    out.wait()


def far(blocks, slots, rights, lefts, needs, sents, tiles, total):
    rows, vectors = rights.shape[2:]
    block_rows = tiles.shape[-1]
    tiles_dir = tiles.shape[1]
    table = tiles.reshape(-1, block_rows, block_rows)
    any_spec = pl.BlockSpec(memory_space=pl.ANY)
    dma = pltpu.SemaphoreType.DMA
    return pl.pallas_call(
        functools.partial(far_kernel, blocks, blocks * slots, tiles_dir),
        out_shape=jax.ShapeDtypeStruct(total.shape, F32),
        in_specs=[any_spec, pl.BlockSpec(memory_space=pltpu.VMEM)] + [any_spec] * 4,
        out_specs=any_spec,
        scratch_shapes=[
            pltpu.SMEM((8,) + needs.shape[2:], I32),
            pltpu.SMEM((16,) + sents.shape[2:], I32),
            pltpu.SMEM((2 * 8 * 2 * blocks * slots + 8 * GROUP,), I32),
            pltpu.VMEM((table.shape[0] + 1, block_rows, block_rows), BF16),
            pltpu.VMEM((DEPTH, 2 * GROUP * block_rows, vectors), BF16),
            pltpu.VMEM((GROUP * block_rows, vectors), BF16),
            pltpu.VMEM(total.shape, F32),
            dma((26,)), dma((DEPTH, 2 * GROUP)),
        ],
        compiler_params=pltpu.CompilerParams(vmem_limit_bytes=28 << 20),
        name="far",
    )(rights, pltpu.with_memory_space_constraint(lefts, pltpu.VMEM), needs, sents, table, total)


LANES = ((0, 1, (1, 0, 2)), (1, 1, (0, 2, 1)), (2, 2, (2, 1, 0)))


def reduce_kernel(scale, total_ref, out_ref, got_core, half, final, last, *rest):
    stages, (send, recv) = rest[:-2], rest[-2:]
    me = lax.axis_index("rows")
    core = me % 2
    twin = other_core(me)

    def at(axis, n):
        c = coord(me, axis)
        return me + STRIDE[axis] * ((c + n) % 4 - c)

    peers = [twin] + [at(axis, n) for axis in range(3) for n in range(1, 4)]
    barrier = pltpu.get_barrier_semaphore()
    for peer in peers:
        pl.semaphore_signal(barrier, inc=1, device_id=(peer,), device_id_type=MESH)
    pl.semaphore_wait(barrier, len(peers))

    def copy(n, src, dst, peer):
        return pltpu.make_async_remote_copy(
            src_ref=src, dst_ref=dst, send_sem=send.at[n], recv_sem=recv.at[n], device_id=(peer,), device_id_type=MESH
        )

    swap = copy(0, total_ref.at[1 - core], got_core, twin)
    swap.start()
    swap.wait()
    half[...] = ((total_ref[core] + got_core[...]) * scale).reshape(half.shape)

    unit = half.shape[-1] // 4
    everything = slice(None)
    held = []
    for first, lanes, order in LANES:
        held.append(([2, 1, 0], half.at[:, :, :, :, pl.ds(first * unit, lanes * unit)]))
    for stage in range(3):
        started = []
        for p, (first, lanes, order) in enumerate(LANES):
            dims, ref = held[p]
            axis = order[stage]
            skip = (everything,) * dims.index(axis)
            got = stages[2 * (3 * p + stage)]
            for n in (2, 1, 3):
                theirs = (coord(me, axis) + n) % 4
                sending = copy(1 + 9 * p + 3 * stage + n - 1, ref.at[skip + (theirs,)], got.at[n - 1], at(axis, n))
                sending.start()
                started.append((p, sending))
        for p, (first, lanes, order) in enumerate(LANES):
            dims, ref = held[p]
            axis = order[stage]
            skip = (everything,) * dims.index(axis)
            got, into = stages[2 * (3 * p + stage)], stages[2 * (3 * p + stage) + 1]
            for q, sending in started:
                if q == p:
                    sending.wait()
            summed = ref[skip + (coord(me, axis),)] + got[0] + got[1] + got[2]
            if stage == 2:
                final[:, first * unit : (first + lanes) * unit] = summed
            else:
                into[...] = summed
            held[p] = ([a for a in dims if a != axis], into)
    give = copy(28, final, last, twin)
    give.start()
    give.wait()
    keep = final.shape[0] // 2
    mine, other = final[...], last[...]
    out_ref[0] = jnp.where(core == 0, mine[:keep], other[keep:])
    out_ref[1] = jnp.where(core == 0, other[:keep], mine[keep:])


def reduce(total, scale, devices):
    _, vectors, width = total.shape
    rows = 2 * vectors // devices
    vm = pl.BlockSpec(memory_space=pltpu.VMEM)
    stages = []
    for _, lanes, _ in LANES:
        for stage in range(3):
            shape = (4,) * (2 - stage) + (rows, lanes * width // 4)
            stages += [pltpu.VMEM((3,) + shape, F32), pltpu.VMEM(shape, F32)]
    return pl.pallas_call(
        functools.partial(reduce_kernel, scale),
        out_shape=jax.ShapeDtypeStruct((2, rows // 2, width), F32),
        in_specs=[vm],
        out_specs=vm,
        scratch_shapes=[
            pltpu.VMEM((vectors, width), F32),
            pltpu.VMEM((4, 4, 4, rows, width), F32),
            pltpu.VMEM((rows, width), F32),
            pltpu.VMEM((rows, width), F32),
            *stages,
            pltpu.SemaphoreType.DMA((29,)),
            pltpu.SemaphoreType.DMA((29,)),
        ],
        compiler_params=pltpu.CompilerParams(
            collective_id=1, has_side_effects=True, vmem_limit_bytes=32 << 20
        ),
        name="reduce",
    )(total)


def needs_of(source_blocks, tile_index, blocks, tiles_dir):
    me = lax.axis_index("rows")
    far_slot = jnp.maximum(source_blocks - blocks, 0)
    peer, copy = far_slot // 2, far_slot % 2
    differ = peer ^ me
    low = [(differ // STRIDE[axis]) % 2 for axis in range(3)]
    high = [(differ // (2 * STRIDE[axis])) % 2 for axis in range(3)]
    left_unit = high[0] + 2 * high[1] + 4 * high[2]
    right_unit = (low[0] ^ high[0]) + 2 * (low[1] ^ high[1]) + 4 * (low[2] ^ high[2])
    provider = (differ % 2) * 8 + right_unit
    block = jnp.arange(blocks, dtype=I32)[None, None, :]
    word = ((block * 16 + provider) * 2 + copy) * tiles_dir + jnp.maximum(tile_index, 0) + 1
    live = jnp.logical_and(tile_index >= 0, source_blocks >= blocks)
    unit = jnp.where(live, left_unit, -1)
    rows = jnp.stack([unit, word // 256, word % 256, jnp.zeros_like(word)])
    return rows.astype(F32).swapaxes(2, 3).reshape(8, -1)


def body(left, right, tiles, source_blocks, tile_index, send_blocks):
    block_rows = tiles.shape[-1]
    rows, _ = right.shape
    blocks = rows // block_rows
    devices = lax.axis_size("rows")
    scale = 1.0 / math.sqrt(rows * devices)
    source_blocks, tile_index = source_blocks.swapaxes(1, 2), tile_index.swapaxes(1, 2)
    info = needs_of(source_blocks, tile_index, blocks, tiles.shape[1])
    sent = send_blocks.T
    rights, lefts, needs, sents, total = gather(left, right, tiles, source_blocks, tile_index, info, sent)
    total = far(blocks, source_blocks.shape[1], rights, lefts, needs, sents, tiles, total)
    return reduce(total, scale, devices)


def solution(mesh):
    placed = (
        P("rows", None),
        P("rows", None),
        P(),
        P(None, "rows", None),
        P(None, "rows", None),
        P("rows", None),
    )
    return jax.shard_map(
        body, mesh=mesh, in_specs=placed, out_specs=P(None, "rows", None), check_vma=False
    )
```

```python
import functools
import math

import jax
import jax.numpy as jnp
from jax import lax
from jax.experimental import pallas as pl
from jax.experimental.pallas import tpu as pltpu
from jax.sharding import PartitionSpec as P

MESH = pl.DeviceIdType.MESH
BF16, F32, I32 = jnp.bfloat16, jnp.float32, jnp.int32

STRIDE = (2, 8, 32)


def coord(me, axis):
    return (me // STRIDE[axis]) % 4


def right_mate(me, axis):
    return me + STRIDE[axis] * (1 - 2 * (coord(me, axis) % 2))


def left_mate(me, axis):
    return me + STRIDE[axis] * (3 - 2 * coord(me, axis))


def other_core(me):
    return me + 1 - 2 * (me % 2)


def cut(rows, unit):
    third = rows // unit // 3
    sizes = [rows - 2 * third * unit, third * unit, third * unit]
    starts = [0, sizes[0], sizes[0] + sizes[1]]
    return list(zip(starts, sizes))


class Cube:
    def __init__(self, own, held, parts, mates, send, recv):
        self.own, self.held, self.parts, self.mates = own, held, parts, mates
        self.send, self.recv = send, recv

    def part(self, unit, p):
        start, size = self.parts[p]
        ref = self.own if unit == 0 else self.held.at[unit]
        return ref.at[pl.ds(start, size)]

    def hop(self, p, unit, axis):
        start, size = self.parts[p]
        into = unit + (1 << axis)
        at = p * 8 + into
        return pltpu.make_async_remote_copy(
            src_ref=self.part(unit, p),
            dst_ref=self.held.at[into].at[pl.ds(start, size)],
            send_sem=self.send.at[at],
            recv_sem=self.recv.at[at],
            device_id=(self.mates[axis],),
            device_id_type=MESH,
        )

    def order(self, p):
        return [(p + n) % 3 for n in range(3)]

    def phases(self):
        result = [[] for _ in range(7)]
        for p in range(len(self.parts)):
            a, b, c = self.order(p)
            ua, ub = 1 << a, 1 << b
            for n, (unit, axis) in enumerate(
                [(0, a), (0, b), (ua, b), (0, c), (ua, c), (ub, c), (ua + ub, c)]
            ):
                result[n].append((p, unit, axis))
        return result

    def start_own(self, axis_place):
        for p in range(len(self.parts)):
            self.hop(p, 0, self.order(p)[axis_place]).start()

    def forward(self, p, unit, axis):
        got = unit + (1 << axis)
        order = self.order(p)
        for later in order[order.index(axis) + 1 :]:
            self.hop(p, got, later).start()

    def drain(self):
        for phase in self.phases():
            for hop in phase:
                self.hop(*hop).wait_send()


def gather_kernel(
    blocks, slots,
    source_ref, tile_ref, left_ref, right_ref, block_ref, tiles_ref, info_ref, sent_ref,
    rights, lefts, needs, sents, total_ref,
    own_right, own_left, own_turned, tile_table, current, total, info, place_of, need_ref,
    local_sem, r_send, r_recv, l_send, l_recv, n_send, n_recv, s_send, s_recv, c_send, c_recv, d_send, d_recv,
):
    me = lax.axis_index("rows")
    right_mates = [right_mate(me, axis) for axis in range(3)]
    left_mates = [left_mate(me, axis) for axis in range(3)]
    twin = other_core(me)

    info_in = pltpu.make_async_copy(info_ref, info, local_sem.at[5])
    info_in.start()
    barrier = pltpu.get_barrier_semaphore()
    for mate in right_mates + left_mates + [twin]:
        pl.semaphore_signal(barrier, inc=1, device_id=(mate,), device_id_type=MESH)

    left_in = pltpu.make_async_copy(left_ref, own_left, local_sem.at[0])
    left_in.start()
    right_in = pltpu.make_async_copy(block_ref, own_right, local_sem.at[1])
    right_in.start()
    tiles_in = pltpu.make_async_copy(tiles_ref, tile_table.at[pl.ds(0, tiles_ref.shape[0])], local_sem.at[2])
    tiles_in.start()
    pl.semaphore_wait(barrier, 7)

    rows = right_ref.shape[0]
    turned_rows = own_turned.shape[0]
    right_cube = Cube(right_ref, rights.at[0], cut(rows, 16), right_mates, r_send, r_recv)
    left_cube = Cube(own_turned, lefts, cut(turned_rows, 16), left_mates, l_send, l_recv)
    need_cube = Cube(need_ref, needs, [(0, need_ref.shape[0])], left_mates, n_send, n_recv)
    sent_cube = Cube(sent_ref, sents.at[0], [(0, sent_ref.shape[0])], right_mates, s_send, s_recv)

    def across(p, unit):
        start, size = right_cube.parts[p]
        at = p * 8 + unit
        return pltpu.make_async_remote_copy(
            src_ref=right_cube.part(unit, p),
            dst_ref=rights.at[1].at[unit].at[pl.ds(start, size)],
            send_sem=c_send.at[at], recv_sem=c_recv.at[at], device_id=(twin,), device_id_type=MESH,
        )

    def across_sent(unit):
        return pltpu.make_async_remote_copy(
            src_ref=sent_cube.part(unit, 0), dst_ref=sents.at[1].at[unit],
            send_sem=d_send.at[unit], recv_sem=d_recv.at[unit], device_id=(twin,), device_id_type=MESH,
        )

    for place in range(3):
        right_cube.start_own(place)
    for place in range(3):
        sent_cube.start_own(place)
    across_sent(0).start()
    for p in range(3):
        across(p, 0).start()

    left_in.wait()
    block_rows = left_ref.shape[0] // blocks
    vectors = left_ref.shape[1]

    def turn(b, _):
        at = pl.multiple_of(b * block_rows, block_rows)
        to = pl.multiple_of(b * vectors, vectors)
        own_turned[pl.ds(to, vectors), :] = own_left[pl.ds(at, block_rows), :].T
        return 0

    lax.fori_loop(0, blocks, turn, 0)
    for place in range(3):
        left_cube.start_own(place)
    left_out = pltpu.make_async_copy(own_turned, lefts.at[0], local_sem.at[3])
    left_out.start()
    right_out = pltpu.make_async_copy(right_ref, rights.at[0].at[0], local_sem.at[4])
    right_out.start()
    sent_out = pltpu.make_async_copy(sent_ref, sents.at[0].at[0], local_sem.at[6])
    sent_out.start()

    info_in.wait()
    many = info.shape[1]
    down = lax.broadcasted_iota(I32, (many, many), 0)
    upto = jnp.where(down <= lax.broadcasted_iota(I32, (many, many), 1), 1.0, 0.0).astype(BF16)
    eight = lax.broadcasted_iota(I32, (8, many), 0)
    for d in range(2):
        mine = jnp.broadcast_to(info[d : d + 1, :], (8, many)) == eight.astype(F32)
        ranks = jnp.dot(jnp.where(mine, 1.0, 0.0).astype(BF16), upto, preferred_element_type=F32)
        place_of[...] = jnp.where(mine, ranks, 0.0)
        words = jnp.where(eight == 0, info[2 + d : 3 + d, :], jnp.where(eight == 1, info[4 + d : 5 + d, :], 0.0))
        words = words.astype(BF16)

        def list_for(unit, _):
            hit = place_of[pl.ds(unit, 1), :] == (down + 1).astype(F32)
            found = lax.dot_general(
                words, jnp.where(hit, 1.0, 0.0).astype(BF16), (((1,), (1,)), ((), ())), preferred_element_type=F32
            )
            word = (found[0:1] * 256.0 + found[1:2]).astype(I32)
            for line in range(many // 128):
                need_ref[unit, pl.ds(d * (many // 128) + line, 1), :] = word[:, line * 128 : line * 128 + 128]
            return 0

        lax.fori_loop(0, 8, list_for, 0)
    for place in range(3):
        need_cube.start_own(place)
    need_out = pltpu.make_async_copy(need_ref, needs.at[0], local_sem.at[5])
    need_out.start()

    tiles_in.wait()
    right_in.wait()
    zero_tile = tiles_ref.shape[0]
    tile_table[zero_tile] = jnp.zeros(tile_table.shape[1:], BF16)
    total[...] = jnp.zeros_like(total)
    group = 8
    groups = blocks // group

    def own_group(n, _):
        d = n // groups
        first = (n % groups) * group

        def row(e, _):
            b = first + e
            summed = jnp.zeros((block_rows, vectors), F32)
            for k0 in range(0, slots, 4):
                chosen, picked = [], []
                for k in range(k0, k0 + 4):
                    chosen.append(tile_table[tile_ref[d, k, b]])
                    picked.append(own_right[source_ref[d, k, b]])
                summed = summed + jnp.dot(
                    jnp.concatenate(chosen, axis=1), jnp.concatenate(picked, axis=0), preferred_element_type=F32
                )
            current[pl.ds(pl.multiple_of(e * block_rows, block_rows), block_rows), :] = summed.astype(BF16)
            return 0

        lax.fori_loop(0, group, row, 0)
        turned = jnp.concatenate(
            [own_turned[pl.ds(pl.multiple_of((first + e) * vectors, vectors), vectors), :] for e in range(group)], axis=1
        )
        total[d] = total[d] + jnp.dot(turned, current[...], preferred_element_type=F32)
        return 0

    def compute(lo, hi):
        lax.fori_loop(lo, hi, own_group, 0)

    plan = {0: (0, 3), 1: (3, 5), 2: (5, 8)}
    phases = list(zip(right_cube.phases(), left_cube.phases()))
    small = list(zip(need_cube.phases(), sent_cube.phases()))
    for n in range(7):
        if n in plan:
            compute(*plan[n])
        if n == 3:
            total_out = pltpu.make_async_copy(total, total_ref, local_sem.at[7])
            total_out.start()
        for hop in small[n][0]:
            need_cube.hop(*hop).wait_recv()
            need_cube.forward(*hop)
        for hop in small[n][1]:
            sent_cube.hop(*hop).wait_recv()
            sent_cube.forward(*hop)
            across_sent(hop[1] + (1 << hop[2])).start()
        for hop, lhop in zip(*phases[n]):
            right_cube.hop(*hop).wait_recv()
            right_cube.forward(*hop)
            across(hop[0], hop[1] + (1 << hop[2])).start()
            left_cube.hop(*lhop).wait_recv()
            left_cube.forward(*lhop)
    for cube in (right_cube, left_cube, need_cube, sent_cube):
        cube.drain()
    for unit in range(8):
        across_sent(unit).wait()
        for p in range(3):
            across(p, unit).wait()
    for copy in (left_out, right_out, need_out, sent_out, total_out):
        copy.wait()


def gather(left, right, tiles, source_blocks, tile_index, info, sent):
    rows, vectors = right.shape
    block_rows = tiles.shape[-1]
    blocks = rows // block_rows
    table = tiles.reshape(-1, block_rows, block_rows)
    offset = jnp.arange(2, dtype=I32)[:, None, None] * tiles.shape[1]
    own = jnp.logical_and(tile_index >= 0, source_blocks < blocks)
    tile_index = jnp.where(own, tile_index + offset, table.shape[0])
    source_blocks = jnp.where(own, source_blocks, 0)
    any_spec = pl.BlockSpec(memory_space=pl.ANY)
    smem = pl.BlockSpec(memory_space=pltpu.SMEM)
    dma = pltpu.SemaphoreType.DMA
    return pl.pallas_call(
        functools.partial(gather_kernel, blocks, source_blocks.shape[1]),
        out_shape=(
            jax.ShapeDtypeStruct((2, 8, rows, vectors), BF16),
            pltpu.VMEM((8, blocks * vectors, block_rows), BF16),
            jax.ShapeDtypeStruct((8, 8) + (2 * info.shape[1] // 128, 128), I32),
            jax.ShapeDtypeStruct((2, 8) + sent.shape, I32),
            jax.ShapeDtypeStruct((2, vectors, vectors), F32),
        ),
        in_specs=[smem, smem] + [any_spec] * 6,
        out_specs=(any_spec, pl.BlockSpec(memory_space=pltpu.VMEM)) + (any_spec,) * 3,
        scratch_shapes=[
            pltpu.VMEM((blocks, block_rows, vectors), BF16),
            pltpu.VMEM((rows, vectors), BF16),
            pltpu.VMEM((blocks * vectors, block_rows), BF16),
            pltpu.VMEM((table.shape[0] + 1, block_rows, block_rows), BF16),
            pltpu.VMEM((8 * block_rows, vectors), BF16),
            pltpu.VMEM((2, vectors, vectors), F32),
            pltpu.VMEM(info.shape, F32),
            pltpu.VMEM(info.shape, F32),
            pltpu.VMEM((8, 2 * info.shape[1] // 128, 128), I32),
            dma((8,)),
            dma((24,)), dma((24,)), dma((24,)), dma((24,)),
            dma((8,)), dma((8,)), dma((8,)), dma((8,)),
            dma((24,)), dma((24,)), dma((8,)), dma((8,)),
        ],
        compiler_params=pltpu.CompilerParams(
            collective_id=0, has_side_effects=True, vmem_limit_bytes=28 << 20
        ),
        name="gather",
    )(source_blocks, tile_index, left, right, right.reshape(blocks, block_rows, vectors), table, info, sent)


GROUP = 16
DEPTH = 4


def far_kernel(
    blocks, many, tiles_dir,
    rights, lefts, needs, sents, tiles_ref, total_in, total_ref,
    need_s, sent_s, terms, order, tile_table, right_buf, current, total, sem, rsem,
):
    me = lax.axis_index("rows")
    block_rows, vectors = right_buf.shape[-2] // GROUP, right_buf.shape[-1]
    copies = [pltpu.make_async_copy(tiles_ref, tile_table.at[pl.ds(0, tiles_ref.shape[0])], sem.at[0])]
    copies.append(pltpu.make_async_copy(total_in, total, sem.at[1]))
    for j in range(8):
        copies.append(pltpu.make_async_copy(needs.at[j, j], need_s.at[j], sem.at[2 + j]))
    for c in range(2):
        for i in range(8):
            copies.append(pltpu.make_async_copy(sents.at[c, i], sent_s.at[c * 8 + i], sem.at[10 + c * 8 + i]))
    for copy in copies[2:] + copies[:2]:
        copy.start()
    for copy in copies[2:]:
        copy.wait()

    zero_tile = 2 * tiles_dir
    tile_bits = (tiles_dir - 1).bit_length()
    block_bits = (blocks - 1).bit_length()
    ADDR, ROW = 8, 8 + 4 + block_bits
    UNROLL = 4

    most = 8 * many
    single_most = 8 * blocks + 3 * GROUP
    pair_at = [d * (most + 2 * GROUP) for d in range(2)]
    single_at = [2 * (most + 2 * GROUP) + d * single_most for d in range(2)]

    def list_dir(d):
        def unit(j, state):
            z, x, y = coord(me, 0), coord(me, 1), coord(me, 2)
            z = jnp.where(j & 1 == 1, 3 - z, z)
            x = jnp.where(j & 2 == 2, 3 - x, x)
            y = jnp.where(j & 4 == 4, 3 - y, y)
            holder = y * STRIDE[2] + x * STRIDE[1] + z * STRIDE[0] + me % 2
            base = d * (many // 128)

            def word(k):
                return need_s[j, base + (k >> 7), k & 127]

            def more(state):
                k, pair, single, last, first = state
                for u in range(UNROLL):
                    w = word(k + u)
                    live = jnp.minimum(w, 1)
                    v = jnp.maximum(w - 1, 0)
                    slot = (v >> tile_bits) & 31
                    block = jnp.maximum(sent_s[slot >> 1, slot & 1, holder], 0)
                    b = v >> (tile_bits + 5)
                    address = ((slot >> 1) << block_bits) + block
                    term = (((j << block_bits) + b) << ROW) + (address << ADDR) + d * tiles_dir + (v & (tiles_dir - 1))
                    second = jnp.where(b == last, live, 0)
                    terms[single] = term
                    terms[pair] = first
                    terms[pair + 1] = term
                    pair = pair + 2 * second
                    single = single + live - 2 * second
                    first = term
                    last = jnp.where(second == 1, -1, b)
                return k + UNROLL, pair, single, last, first

            def going(state):
                k = state[0]
                return jnp.logical_and(k < many, word(jnp.minimum(k, many - 1)) > 0)

            return lax.while_loop(going, more, (jnp.int32(0), *state, jnp.int32(-1), jnp.int32(0)))[1:3]

        ends = lax.fori_loop(0, 8, unit, (jnp.int32(pair_at[d]), jnp.int32(single_at[d])))
        counts = []
        for end, first in zip(ends, (pair_at[d], single_at[d])):
            for u in range(GROUP):
                terms[end + u] = zero_tile
            counts.append((end - first + GROUP - 1) // GROUP)
        return counts

    count = jnp.int32(0)
    for d in range(2):
        for kind, (many_groups, first) in enumerate(zip(list_dir(d), (pair_at[d], single_at[d]))):

            def note(n, _, kind=kind, first=first, d=d, count=count):
                order[count + n] = ((first + n * GROUP) << 2) + d * 2 + kind
                return 0

            lax.fori_loop(0, many_groups, note, 0)
            count = count + many_groups

    def start(g):
        at = order[g] >> 2
        slot = g % DEPTH
        for e in range(GROUP):
            address = (terms[at + e] >> ADDR) & ((16 << block_bits) - 1)
            provider, block = address >> block_bits, address & (blocks - 1)
            pltpu.make_async_copy(
                rights.at[provider >> 3, provider & 7, pl.ds(pl.multiple_of(block * block_rows, block_rows), block_rows)],
                right_buf.at[slot, pl.ds(e * block_rows, block_rows)],
                rsem.at[slot],
            ).start()

    for g in range(DEPTH - 1):
        @pl.when(g < count)
        def _():
            start(g)

    for copy in copies[:2]:
        copy.wait()
    tile_table[zero_tile] = jnp.zeros(tile_table.shape[1:], BF16)

    def left_of(term):
        row = term >> ROW
        return lefts[row >> block_bits, pl.ds(pl.multiple_of((row & (blocks - 1)) * vectors, vectors), vectors), :]

    def step(g, _):
        @pl.when(g + DEPTH - 1 < count)
        def _():
            start(g + DEPTH - 1)

        word = order[g]
        at, d = word >> 2, (word >> 1) & 1
        slot = g % DEPTH
        pltpu.make_async_copy(right_buf.at[slot], right_buf.at[slot], rsem.at[slot]).wait()
        for kind, width in ((0, 2), (1, 1)):

            @pl.when(word & 1 == kind)
            def _(width=width):
                turned = []
                for n, e in enumerate(range(0, GROUP, width)):
                    chosen = [tile_table[terms[at + e + u] & 255] for u in range(width)]
                    current[pl.ds(n * block_rows, block_rows), :] = jnp.dot(
                        jnp.concatenate(chosen, axis=1) if width > 1 else chosen[0],
                        right_buf[slot, pl.ds(e * block_rows, width * block_rows), :],
                        preferred_element_type=F32,
                    ).astype(BF16)
                    turned.append(left_of(terms[at + e]))
                total[d] = total[d] + jnp.dot(
                    jnp.concatenate(turned, axis=1),
                    current[pl.ds(0, len(turned) * block_rows), :],
                    preferred_element_type=F32,
                )

        return 0

    lax.fori_loop(0, count, step, 0)
    out = pltpu.make_async_copy(total, total_ref, sem.at[0])
    out.start()
    out.wait()


def far(blocks, slots, rights, lefts, needs, sents, tiles, total):
    rows, vectors = rights.shape[2:]
    block_rows = tiles.shape[-1]
    tiles_dir = tiles.shape[1]
    table = tiles.reshape(-1, block_rows, block_rows)
    any_spec = pl.BlockSpec(memory_space=pl.ANY)
    dma = pltpu.SemaphoreType.DMA
    return pl.pallas_call(
        functools.partial(far_kernel, blocks, blocks * slots, tiles_dir),
        out_shape=jax.ShapeDtypeStruct(total.shape, F32),
        in_specs=[any_spec, pl.BlockSpec(memory_space=pltpu.VMEM)] + [any_spec] * 4,
        out_specs=any_spec,
        scratch_shapes=[
            pltpu.SMEM((8,) + needs.shape[2:], I32),
            pltpu.SMEM((16,) + sents.shape[2:], I32),
            pltpu.SMEM((2 * (8 * blocks * slots + 2 * GROUP + 8 * blocks + 3 * GROUP),), I32),
            pltpu.SMEM((2 * (8 * blocks * slots + 8 * blocks) // GROUP + 8,), I32),
            pltpu.VMEM((table.shape[0] + 1, block_rows, block_rows), BF16),
            pltpu.VMEM((DEPTH, GROUP * block_rows, vectors), BF16),
            pltpu.VMEM((GROUP * block_rows, vectors), BF16),
            pltpu.VMEM(total.shape, F32),
            dma((26,)), dma((DEPTH,)),
        ],
        compiler_params=pltpu.CompilerParams(vmem_limit_bytes=28 << 20),
        name="far",
    )(rights, pltpu.with_memory_space_constraint(lefts, pltpu.VMEM), needs, sents, table, total)


LANES = ((0, 1, (1, 0, 2)), (1, 1, (0, 2, 1)), (2, 2, (2, 1, 0)))


def reduce_kernel(scale, total_ref, out_ref, mine_core, local_sem, got_core, half, final, last, *rest):
    stages, (send, recv) = rest[:-2], rest[-2:]
    me = lax.axis_index("rows")
    core = me % 2
    twin = other_core(me)

    def at(axis, n):
        c = coord(me, axis)
        return me + STRIDE[axis] * ((c + n) % 4 - c)

    mine_in = pltpu.make_async_copy(total_ref.at[core], mine_core, local_sem)
    mine_in.start()
    peers = [twin] + [at(axis, n) for axis in range(3) for n in range(1, 4)]
    barrier = pltpu.get_barrier_semaphore()
    for peer in peers:
        pl.semaphore_signal(barrier, inc=1, device_id=(peer,), device_id_type=MESH)
    pl.semaphore_wait(barrier, len(peers))

    def copy(n, src, dst, peer):
        return pltpu.make_async_remote_copy(
            src_ref=src, dst_ref=dst, send_sem=send.at[n], recv_sem=recv.at[n], device_id=(peer,), device_id_type=MESH
        )

    swap = copy(0, total_ref.at[1 - core], got_core, twin)
    swap.start()
    mine_in.wait()
    swap.wait()
    half[...] = ((mine_core[...] + got_core[...]) * scale).reshape(half.shape)

    unit = half.shape[-1] // 4
    everything = slice(None)
    held = []
    for first, lanes, order in LANES:
        held.append(([2, 1, 0], half.at[:, :, :, :, pl.ds(first * unit, lanes * unit)]))
    for stage in range(3):
        started = []
        for p, (first, lanes, order) in enumerate(LANES):
            dims, ref = held[p]
            axis = order[stage]
            skip = (everything,) * dims.index(axis)
            got = stages[2 * (3 * p + stage)]
            for n in (2, 1, 3):
                theirs = (coord(me, axis) + n) % 4
                sending = copy(1 + 9 * p + 3 * stage + n - 1, ref.at[skip + (theirs,)], got.at[n - 1], at(axis, n))
                sending.start()
                started.append((p, sending))
        for p, (first, lanes, order) in enumerate(LANES):
            dims, ref = held[p]
            axis = order[stage]
            skip = (everything,) * dims.index(axis)
            got, into = stages[2 * (3 * p + stage)], stages[2 * (3 * p + stage) + 1]
            for q, sending in started:
                if q == p:
                    sending.wait()
            summed = ref[skip + (coord(me, axis),)] + got[0] + got[1] + got[2]
            if stage == 2:
                final[:, first * unit : (first + lanes) * unit] = summed
            else:
                into[...] = summed
            held[p] = ([a for a in dims if a != axis], into)
    give = copy(28, final, last, twin)
    give.start()
    give.wait()
    keep = final.shape[0] // 2
    mine, other = final[...], last[...]
    out_ref[0] = jnp.where(core == 0, mine[:keep], other[keep:])
    out_ref[1] = jnp.where(core == 0, other[:keep], mine[keep:])


def reduce(total, scale, devices):
    _, vectors, width = total.shape
    rows = 2 * vectors // devices
    vm = pl.BlockSpec(memory_space=pltpu.VMEM)
    stages = []
    for _, lanes, _ in LANES:
        for stage in range(3):
            shape = (4,) * (2 - stage) + (rows, lanes * width // 4)
            stages += [pltpu.VMEM((3,) + shape, F32), pltpu.VMEM(shape, F32)]
    return pl.pallas_call(
        functools.partial(reduce_kernel, scale),
        out_shape=jax.ShapeDtypeStruct((2, rows // 2, width), F32),
        in_specs=[pl.BlockSpec(memory_space=pl.ANY)],
        out_specs=vm,
        scratch_shapes=[
            pltpu.VMEM((vectors, width), F32),
            pltpu.SemaphoreType.DMA,
            pltpu.VMEM((vectors, width), F32),
            pltpu.VMEM((4, 4, 4, rows, width), F32),
            pltpu.VMEM((rows, width), F32),
            pltpu.VMEM((rows, width), F32),
            *stages,
            pltpu.SemaphoreType.DMA((29,)),
            pltpu.SemaphoreType.DMA((29,)),
        ],
        compiler_params=pltpu.CompilerParams(
            collective_id=1, has_side_effects=True, vmem_limit_bytes=32 << 20
        ),
        name="reduce",
    )(pltpu.with_memory_space_constraint(total, pltpu.HBM))


def needs_of(source_blocks, tile_index, blocks, tiles_dir):
    me = lax.axis_index("rows")
    far_slot = jnp.maximum(source_blocks - blocks, 0)
    peer, copy = far_slot // 2, far_slot % 2
    differ = peer ^ me
    low = [(differ // STRIDE[axis]) % 2 for axis in range(3)]
    high = [(differ // (2 * STRIDE[axis])) % 2 for axis in range(3)]
    left_unit = high[0] + 2 * high[1] + 4 * high[2]
    right_unit = (low[0] ^ high[0]) + 2 * (low[1] ^ high[1]) + 4 * (low[2] ^ high[2])
    provider = (differ % 2) * 8 + right_unit
    block = jnp.arange(blocks, dtype=I32)[None, None, :]
    word = ((block * 16 + provider) * 2 + copy) * tiles_dir + jnp.maximum(tile_index, 0) + 1
    live = jnp.logical_and(tile_index >= 0, source_blocks >= blocks)
    unit = jnp.where(live, left_unit, -1)
    rows = jnp.stack([unit, word // 256, word % 256, jnp.zeros_like(word)])
    return rows.astype(F32).swapaxes(2, 3).reshape(8, -1)


def body(left, right, tiles, source_blocks, tile_index, send_blocks):
    block_rows = tiles.shape[-1]
    rows, _ = right.shape
    blocks = rows // block_rows
    devices = lax.axis_size("rows")
    scale = 1.0 / math.sqrt(rows * devices)
    source_blocks, tile_index = source_blocks.swapaxes(1, 2), tile_index.swapaxes(1, 2)
    info = needs_of(source_blocks, tile_index, blocks, tiles.shape[1])
    sent = send_blocks.T
    rights, lefts, needs, sents, total = gather(left, right, tiles, source_blocks, tile_index, info, sent)
    total = far(blocks, source_blocks.shape[1], rights, lefts, needs, sents, tiles, total)
    return reduce(total, scale, devices)


def solution(mesh):
    placed = (
        P("rows", None),
        P("rows", None),
        P(),
        P(None, "rows", None),
        P(None, "rows", None),
        P("rows", None),
    )
    return jax.shard_map(
        body, mesh=mesh, in_specs=placed, out_specs=P(None, "rows", None), check_vma=False
    )
```

```python
import functools
import math

import jax
import jax.numpy as jnp
from jax import lax
from jax.experimental import pallas as pl
from jax.experimental.pallas import tpu as pltpu
from jax.sharding import PartitionSpec as P

MESH = pl.DeviceIdType.MESH
BF16, F32, I32 = jnp.bfloat16, jnp.float32, jnp.int32

STRIDE = (2, 8, 32)


def coord(me, axis):
    return (me // STRIDE[axis]) % 4


def right_mate(me, axis):
    return me + STRIDE[axis] * (1 - 2 * (coord(me, axis) % 2))


def left_mate(me, axis):
    return me + STRIDE[axis] * (3 - 2 * coord(me, axis))


def other_core(me):
    return me + 1 - 2 * (me % 2)


def cut(rows, unit):
    third = rows // unit // 3
    sizes = [rows - 2 * third * unit, third * unit, third * unit]
    starts = [0, sizes[0], sizes[0] + sizes[1]]
    return list(zip(starts, sizes))


class Cube:
    def __init__(self, own, held, parts, mates, send, recv):
        self.own, self.held, self.parts, self.mates = own, held, parts, mates
        self.send, self.recv = send, recv

    def part(self, unit, p):
        start, size = self.parts[p]
        ref = self.own if unit == 0 else self.held.at[unit]
        return ref.at[pl.ds(start, size)]

    def hop(self, p, unit, axis):
        start, size = self.parts[p]
        into = unit + (1 << axis)
        at = p * 8 + into
        return pltpu.make_async_remote_copy(
            src_ref=self.part(unit, p),
            dst_ref=self.held.at[into].at[pl.ds(start, size)],
            send_sem=self.send.at[at],
            recv_sem=self.recv.at[at],
            device_id=(self.mates[axis],),
            device_id_type=MESH,
        )

    def order(self, p):
        return [(p + n) % 3 for n in range(3)]

    def phases(self):
        result = [[] for _ in range(7)]
        for p in range(len(self.parts)):
            a, b, c = self.order(p)
            ua, ub = 1 << a, 1 << b
            for n, (unit, axis) in enumerate(
                [(0, a), (0, b), (ua, b), (0, c), (ua, c), (ub, c), (ua + ub, c)]
            ):
                result[n].append((p, unit, axis))
        return result

    def start_own(self, axis_place):
        for p in range(len(self.parts)):
            self.hop(p, 0, self.order(p)[axis_place]).start()

    def forward(self, p, unit, axis):
        got = unit + (1 << axis)
        order = self.order(p)
        for later in order[order.index(axis) + 1 :]:
            self.hop(p, got, later).start()

    def drain(self):
        for phase in self.phases():
            for hop in phase:
                self.hop(*hop).wait_send()


def gather_kernel(
    blocks, slots,
    source_ref, tile_ref, left_ref, right_ref, block_ref, tiles_ref, info_ref, sent_ref,
    rights, lefts, needs, sents, total_ref,
    own_right, own_left, own_turned, tile_table, current, total, info, place_of, need_ref,
    local_sem, r_send, r_recv, l_send, l_recv, n_send, n_recv, s_send, s_recv, c_send, c_recv, d_send, d_recv,
):
    me = lax.axis_index("rows")
    right_mates = [right_mate(me, axis) for axis in range(3)]
    left_mates = [left_mate(me, axis) for axis in range(3)]
    twin = other_core(me)

    info_in = pltpu.make_async_copy(info_ref, info, local_sem.at[5])
    info_in.start()
    barrier = pltpu.get_barrier_semaphore()
    for mate in right_mates + left_mates + [twin]:
        pl.semaphore_signal(barrier, inc=1, device_id=(mate,), device_id_type=MESH)

    left_in = pltpu.make_async_copy(left_ref, own_left, local_sem.at[0])
    left_in.start()
    right_in = pltpu.make_async_copy(block_ref, own_right, local_sem.at[1])
    right_in.start()
    tiles_in = pltpu.make_async_copy(tiles_ref, tile_table.at[pl.ds(0, tiles_ref.shape[0])], local_sem.at[2])
    tiles_in.start()
    pl.semaphore_wait(barrier, 7)

    rows = right_ref.shape[0]
    turned_rows = own_turned.shape[0]
    right_cube = Cube(right_ref, rights.at[0], cut(rows, 16), right_mates, r_send, r_recv)
    left_cube = Cube(own_turned, lefts, cut(turned_rows, 16), left_mates, l_send, l_recv)
    need_cube = Cube(need_ref, needs, [(0, need_ref.shape[0])], left_mates, n_send, n_recv)
    sent_cube = Cube(sent_ref, sents.at[0], [(0, sent_ref.shape[0])], right_mates, s_send, s_recv)

    def across(p, unit):
        start, size = right_cube.parts[p]
        at = p * 8 + unit
        return pltpu.make_async_remote_copy(
            src_ref=right_cube.part(unit, p),
            dst_ref=rights.at[1].at[unit].at[pl.ds(start, size)],
            send_sem=c_send.at[at], recv_sem=c_recv.at[at], device_id=(twin,), device_id_type=MESH,
        )

    def across_sent(unit):
        return pltpu.make_async_remote_copy(
            src_ref=sent_cube.part(unit, 0), dst_ref=sents.at[1].at[unit],
            send_sem=d_send.at[unit], recv_sem=d_recv.at[unit], device_id=(twin,), device_id_type=MESH,
        )

    for place in range(3):
        right_cube.start_own(place)
    for place in range(3):
        sent_cube.start_own(place)
    across_sent(0).start()
    for p in range(3):
        across(p, 0).start()

    left_in.wait()
    block_rows = left_ref.shape[0] // blocks
    vectors = left_ref.shape[1]

    def turn(b, _):
        at = pl.multiple_of(b * block_rows, block_rows)
        to = pl.multiple_of(b * vectors, vectors)
        own_turned[pl.ds(to, vectors), :] = own_left[pl.ds(at, block_rows), :].T
        return 0

    lax.fori_loop(0, blocks, turn, 0)
    for place in range(3):
        left_cube.start_own(place)
    left_out = pltpu.make_async_copy(own_turned, lefts.at[0], local_sem.at[3])
    left_out.start()
    right_out = pltpu.make_async_copy(right_ref, rights.at[0].at[0], local_sem.at[4])
    right_out.start()
    sent_out = pltpu.make_async_copy(sent_ref, sents.at[0].at[0], local_sem.at[6])
    sent_out.start()

    info_in.wait()
    many = info.shape[1]
    down = lax.broadcasted_iota(I32, (many, many), 0)
    upto = jnp.where(down <= lax.broadcasted_iota(I32, (many, many), 1), 1.0, 0.0).astype(BF16)
    eight = lax.broadcasted_iota(I32, (8, many), 0)
    for d in range(2):
        mine = jnp.broadcast_to(info[d : d + 1, :], (8, many)) == eight.astype(F32)
        ranks = jnp.dot(jnp.where(mine, 1.0, 0.0).astype(BF16), upto, preferred_element_type=F32)
        place_of[...] = jnp.where(mine, ranks, 0.0)
        words = jnp.where(eight == 0, info[2 + d : 3 + d, :], jnp.where(eight == 1, info[4 + d : 5 + d, :], 0.0))
        words = words.astype(BF16)

        def list_for(unit, _):
            hit = place_of[pl.ds(unit, 1), :] == (down + 1).astype(F32)
            found = lax.dot_general(
                words, jnp.where(hit, 1.0, 0.0).astype(BF16), (((1,), (1,)), ((), ())), preferred_element_type=F32
            )
            word = (found[0:1] * 256.0 + found[1:2]).astype(I32)
            for line in range(many // 128):
                need_ref[unit, pl.ds(d * (many // 128) + line, 1), :] = word[:, line * 128 : line * 128 + 128]
            return 0

        lax.fori_loop(0, 8, list_for, 0)
    for place in range(3):
        need_cube.start_own(place)
    need_out = pltpu.make_async_copy(need_ref, needs.at[0], local_sem.at[5])
    need_out.start()

    tiles_in.wait()
    right_in.wait()
    zero_tile = tiles_ref.shape[0]
    tile_table[zero_tile] = jnp.zeros(tile_table.shape[1:], BF16)
    total[...] = jnp.zeros_like(total)
    group = 8
    groups = blocks // group

    def own_group(n, _):
        d = n // groups
        first = (n % groups) * group

        def row(e, _):
            b = first + e
            summed = jnp.zeros((block_rows, vectors), F32)
            for k0 in range(0, slots, 4):
                chosen, picked = [], []
                for k in range(k0, k0 + 4):
                    chosen.append(tile_table[tile_ref[d, k, b]])
                    picked.append(own_right[source_ref[d, k, b]])
                summed = summed + jnp.dot(
                    jnp.concatenate(chosen, axis=1), jnp.concatenate(picked, axis=0), preferred_element_type=F32
                )
            current[pl.ds(pl.multiple_of(e * block_rows, block_rows), block_rows), :] = summed.astype(BF16)
            return 0

        lax.fori_loop(0, group, row, 0)
        turned = jnp.concatenate(
            [own_turned[pl.ds(pl.multiple_of((first + e) * vectors, vectors), vectors), :] for e in range(group)], axis=1
        )
        total[d] = total[d] + jnp.dot(turned, current[...], preferred_element_type=F32)
        return 0

    def compute(lo, hi):
        lax.fori_loop(lo, hi, own_group, 0)

    plan = {0: (0, 3), 1: (3, 5), 2: (5, 8)}
    phases = list(zip(right_cube.phases(), left_cube.phases()))
    small = list(zip(need_cube.phases(), sent_cube.phases()))
    for n in range(7):
        if n in plan:
            compute(*plan[n])
        if n == 3:
            total_out = pltpu.make_async_copy(total, total_ref, local_sem.at[7])
            total_out.start()
        for hop in small[n][0]:
            need_cube.hop(*hop).wait_recv()
            need_cube.forward(*hop)
        for hop in small[n][1]:
            sent_cube.hop(*hop).wait_recv()
            sent_cube.forward(*hop)
            across_sent(hop[1] + (1 << hop[2])).start()
        for hop, lhop in zip(*phases[n]):
            right_cube.hop(*hop).wait_recv()
            right_cube.forward(*hop)
            across(hop[0], hop[1] + (1 << hop[2])).start()
            left_cube.hop(*lhop).wait_recv()
            left_cube.forward(*lhop)
    for cube in (right_cube, left_cube, need_cube, sent_cube):
        cube.drain()
    for unit in range(8):
        across_sent(unit).wait()
        for p in range(3):
            across(p, unit).wait()
    for copy in (left_out, right_out, need_out, sent_out, total_out):
        copy.wait()


def gather(left, right, tiles, source_blocks, tile_index, info, sent):
    rows, vectors = right.shape
    block_rows = tiles.shape[-1]
    blocks = rows // block_rows
    table = tiles.reshape(-1, block_rows, block_rows)
    offset = jnp.arange(2, dtype=I32)[:, None, None] * tiles.shape[1]
    own = jnp.logical_and(tile_index >= 0, source_blocks < blocks)
    tile_index = jnp.where(own, tile_index + offset, table.shape[0])
    source_blocks = jnp.where(own, source_blocks, 0)
    any_spec = pl.BlockSpec(memory_space=pl.ANY)
    smem = pl.BlockSpec(memory_space=pltpu.SMEM)
    dma = pltpu.SemaphoreType.DMA
    return pl.pallas_call(
        functools.partial(gather_kernel, blocks, source_blocks.shape[1]),
        out_shape=(
            jax.ShapeDtypeStruct((2, 8, rows, vectors), BF16),
            pltpu.VMEM((8, blocks * vectors, block_rows), BF16),
            jax.ShapeDtypeStruct((8, 8) + (2 * info.shape[1] // 128, 128), I32),
            jax.ShapeDtypeStruct((2, 8) + sent.shape, I32),
            jax.ShapeDtypeStruct((2, vectors, vectors), F32),
        ),
        in_specs=[smem, smem] + [any_spec] * 6,
        out_specs=(any_spec, pl.BlockSpec(memory_space=pltpu.VMEM)) + (any_spec,) * 3,
        scratch_shapes=[
            pltpu.VMEM((blocks, block_rows, vectors), BF16),
            pltpu.VMEM((rows, vectors), BF16),
            pltpu.VMEM((blocks * vectors, block_rows), BF16),
            pltpu.VMEM((table.shape[0] + 1, block_rows, block_rows), BF16),
            pltpu.VMEM((8 * block_rows, vectors), BF16),
            pltpu.VMEM((2, vectors, vectors), F32),
            pltpu.VMEM(info.shape, F32),
            pltpu.VMEM(info.shape, F32),
            pltpu.VMEM((8, 2 * info.shape[1] // 128, 128), I32),
            dma((8,)),
            dma((24,)), dma((24,)), dma((24,)), dma((24,)),
            dma((8,)), dma((8,)), dma((8,)), dma((8,)),
            dma((24,)), dma((24,)), dma((8,)), dma((8,)),
        ],
        compiler_params=pltpu.CompilerParams(
            collective_id=0, has_side_effects=True, vmem_limit_bytes=28 << 20
        ),
        name="gather",
    )(source_blocks, tile_index, left, right, right.reshape(blocks, block_rows, vectors), table, info, sent)


GROUP = 16
DEPTH = 4


def far_kernel(
    blocks, many, tiles_dir,
    rights, lefts, needs, sents, tiles_ref, total_in, total_ref,
    need_s, sent_s, terms, order, tile_table, right_buf, current, total, sem, rsem,
):
    me = lax.axis_index("rows")
    block_rows, vectors = right_buf.shape[-2] // GROUP, right_buf.shape[-1]
    copies = [pltpu.make_async_copy(tiles_ref, tile_table.at[pl.ds(0, tiles_ref.shape[0])], sem.at[0])]
    copies.append(pltpu.make_async_copy(total_in, total, sem.at[1]))
    for j in range(8):
        copies.append(pltpu.make_async_copy(needs.at[j, j], need_s.at[j], sem.at[2 + j]))
    for c in range(2):
        for i in range(8):
            copies.append(pltpu.make_async_copy(sents.at[c, i], sent_s.at[c * 8 + i], sem.at[10 + c * 8 + i]))
    for copy in copies[2:] + copies[:2]:
        copy.start()
    for copy in copies[2:]:
        copy.wait()

    zero_tile = 2 * tiles_dir
    tile_bits = (tiles_dir - 1).bit_length()
    block_bits = (blocks - 1).bit_length()
    ADDR, ROW = 8, 8 + 4 + block_bits
    UNROLL = 4

    most = 8 * many
    single_most = 8 * blocks + 3 * GROUP
    pair_at = [d * (most + 2 * GROUP) for d in range(2)]
    single_at = [2 * (most + 2 * GROUP) + d * single_most for d in range(2)]

    def list_dir(d):
        def unit(j, state):
            z, x, y = coord(me, 0), coord(me, 1), coord(me, 2)
            z = jnp.where(j & 1 == 1, 3 - z, z)
            x = jnp.where(j & 2 == 2, 3 - x, x)
            y = jnp.where(j & 4 == 4, 3 - y, y)
            holder = y * STRIDE[2] + x * STRIDE[1] + z * STRIDE[0] + me % 2
            base = d * (many // 128)

            def word(k):
                return need_s[j, base + (k >> 7), k & 127]

            def more(state):
                k, pair, single, last, first = state
                for u in range(UNROLL):
                    w = word(k + u)
                    live = jnp.minimum(w, 1)
                    v = jnp.maximum(w - 1, 0)
                    slot = (v >> tile_bits) & 31
                    block = jnp.maximum(sent_s[slot >> 1, slot & 1, holder], 0)
                    b = v >> (tile_bits + 5)
                    address = ((slot >> 1) << block_bits) + block
                    term = (((j << block_bits) + b) << ROW) + (address << ADDR) + d * tiles_dir + (v & (tiles_dir - 1))
                    second = jnp.where(b == last, live, 0)
                    terms[single] = term
                    terms[pair] = first
                    terms[pair + 1] = term
                    pair = pair + 2 * second
                    single = single + live - 2 * second
                    first = term
                    last = jnp.where(second == 1, -1, b)
                return k + UNROLL, pair, single, last, first

            def going(state):
                k = state[0]
                return jnp.logical_and(k < many, word(jnp.minimum(k, many - 1)) > 0)

            return lax.while_loop(going, more, (jnp.int32(0), *state, jnp.int32(-1), jnp.int32(0)))[1:3]

        ends = lax.fori_loop(0, 8, unit, (jnp.int32(pair_at[d]), jnp.int32(single_at[d])))
        counts = []
        for end, first in zip(ends, (pair_at[d], single_at[d])):
            for u in range(GROUP):
                terms[end + u] = zero_tile
            counts.append((end - first + GROUP - 1) // GROUP)
        return counts

    def start(g):
        at = order[g] >> 2
        slot = g % DEPTH
        for e in range(GROUP):
            address = (terms[at + e] >> ADDR) & ((16 << block_bits) - 1)
            provider, block = address >> block_bits, address & (blocks - 1)
            pltpu.make_async_copy(
                rights.at[provider >> 3, provider & 7, pl.ds(pl.multiple_of(block * block_rows, block_rows), block_rows)],
                right_buf.at[slot, pl.ds(e * block_rows, block_rows)],
                rsem.at[slot],
            ).start()

    count = jnp.int32(0)
    for d in range(2):
        begun = count
        for kind, (many_groups, first) in enumerate(zip(list_dir(d), (pair_at[d], single_at[d]))):

            def note(n, _, kind=kind, first=first, d=d, count=count):
                order[count + n] = ((first + n * GROUP) << 2) + d * 2 + kind
                return 0

            lax.fori_loop(0, many_groups, note, 0)
            count = count + many_groups
        for g in range(DEPTH - 1):

            @pl.when(jnp.logical_and(g >= begun, g < count))
            def _(g=g):
                start(g)

    for copy in copies[:2]:
        copy.wait()
    tile_table[zero_tile] = jnp.zeros(tile_table.shape[1:], BF16)

    def left_of(term):
        row = term >> ROW
        return lefts[row >> block_bits, pl.ds(pl.multiple_of((row & (blocks - 1)) * vectors, vectors), vectors), :]

    def step(g, _):
        @pl.when(g + DEPTH - 1 < count)
        def _():
            start(g + DEPTH - 1)

        word = order[g]
        at, d = word >> 2, (word >> 1) & 1
        slot = g % DEPTH
        pltpu.make_async_copy(right_buf.at[slot], right_buf.at[slot], rsem.at[slot]).wait()
        for kind, width in ((0, 2), (1, 1)):

            @pl.when(word & 1 == kind)
            def _(width=width):
                turned = []
                for n, e in enumerate(range(0, GROUP, width)):
                    chosen = [tile_table[terms[at + e + u] & 255] for u in range(width)]
                    current[pl.ds(n * block_rows, block_rows), :] = jnp.dot(
                        jnp.concatenate(chosen, axis=1) if width > 1 else chosen[0],
                        right_buf[slot, pl.ds(e * block_rows, width * block_rows), :],
                        preferred_element_type=F32,
                    ).astype(BF16)
                    turned.append(left_of(terms[at + e]))
                total[d] = total[d] + jnp.dot(
                    jnp.concatenate(turned, axis=1),
                    current[pl.ds(0, len(turned) * block_rows), :],
                    preferred_element_type=F32,
                )

        return 0

    lax.fori_loop(0, count, step, 0)
    out = pltpu.make_async_copy(total, total_ref, sem.at[0])
    out.start()
    out.wait()


def far(blocks, slots, rights, lefts, needs, sents, tiles, total):
    rows, vectors = rights.shape[2:]
    block_rows = tiles.shape[-1]
    tiles_dir = tiles.shape[1]
    table = tiles.reshape(-1, block_rows, block_rows)
    any_spec = pl.BlockSpec(memory_space=pl.ANY)
    dma = pltpu.SemaphoreType.DMA
    return pl.pallas_call(
        functools.partial(far_kernel, blocks, blocks * slots, tiles_dir),
        out_shape=jax.ShapeDtypeStruct(total.shape, F32),
        in_specs=[any_spec, pl.BlockSpec(memory_space=pltpu.VMEM)] + [any_spec] * 4,
        out_specs=any_spec,
        scratch_shapes=[
            pltpu.SMEM((8,) + needs.shape[2:], I32),
            pltpu.SMEM((16,) + sents.shape[2:], I32),
            pltpu.SMEM((2 * (8 * blocks * slots + 2 * GROUP + 8 * blocks + 3 * GROUP),), I32),
            pltpu.SMEM((2 * (8 * blocks * slots + 8 * blocks) // GROUP + 8,), I32),
            pltpu.VMEM((table.shape[0] + 1, block_rows, block_rows), BF16),
            pltpu.VMEM((DEPTH, GROUP * block_rows, vectors), BF16),
            pltpu.VMEM((GROUP * block_rows, vectors), BF16),
            pltpu.VMEM(total.shape, F32),
            dma((26,)), dma((DEPTH,)),
        ],
        compiler_params=pltpu.CompilerParams(vmem_limit_bytes=28 << 20),
        name="far",
    )(rights, pltpu.with_memory_space_constraint(lefts, pltpu.VMEM), needs, sents, table, total)


LANES = ((2, 2, (2, 1, 0)), (0, 1, (1, 0, 2)), (1, 1, (0, 2, 1)))


def reduce_kernel(scale, total_ref, out_ref, mine_core, local_sem, got_core, half, final, last, *rest):
    stages, (send, recv) = rest[:-2], rest[-2:]
    me = lax.axis_index("rows")
    core = me % 2
    twin = other_core(me)

    def at(axis, n):
        c = coord(me, axis)
        return me + STRIDE[axis] * ((c + n) % 4 - c)

    mine_in = pltpu.make_async_copy(total_ref.at[core], mine_core, local_sem)
    mine_in.start()
    peers = [twin] + [at(axis, n) for axis in range(3) for n in range(1, 4)]
    barrier = pltpu.get_barrier_semaphore()
    for peer in peers:
        pl.semaphore_signal(barrier, inc=1, device_id=(peer,), device_id_type=MESH)
    pl.semaphore_wait(barrier, len(peers))

    def copy(n, src, dst, peer):
        return pltpu.make_async_remote_copy(
            src_ref=src, dst_ref=dst, send_sem=send.at[n], recv_sem=recv.at[n], device_id=(peer,), device_id_type=MESH
        )

    unit = got_core.shape[-1] // 4
    swaps = []
    for p, (first, lanes, order) in enumerate(LANES):
        columns = pl.ds(first * unit, lanes * unit)
        swaps.append(
            copy(28 + p, total_ref.at[1 - core].at[:, columns], got_core.at[:, columns], twin)
        )
        swaps[-1].start()
    mine_in.wait()

    everything = slice(None)
    held = []
    for first, lanes, order in LANES:
        held.append(([2, 1, 0], half.at[:, :, :, :, pl.ds(first * unit, lanes * unit)]))
    for stage in range(3):
        started = []
        for p, (first, lanes, order) in enumerate(LANES):
            dims, ref = held[p]
            axis = order[stage]
            skip = (everything,) * dims.index(axis)
            got = stages[2 * (3 * p + stage)]
            if stage == 0:
                swaps[p].wait()
                columns = slice(first * unit, (first + lanes) * unit)
                both = (mine_core[:, columns] + got_core[:, columns]) * scale
                half[:, :, :, :, columns] = both.reshape(half.shape[:-1] + (lanes * unit,))
            for n in (2, 1, 3):
                theirs = (coord(me, axis) + n) % 4
                sending = copy(1 + 9 * p + 3 * stage + n - 1, ref.at[skip + (theirs,)], got.at[n - 1], at(axis, n))
                sending.start()
                started.append((p, sending))
        for p, (first, lanes, order) in enumerate(LANES):
            dims, ref = held[p]
            axis = order[stage]
            skip = (everything,) * dims.index(axis)
            got, into = stages[2 * (3 * p + stage)], stages[2 * (3 * p + stage) + 1]
            for q, sending in started:
                if q == p:
                    sending.wait()
            summed = ref[skip + (coord(me, axis),)] + got[0] + got[1] + got[2]
            if stage == 2:
                final[:, first * unit : (first + lanes) * unit] = summed
            else:
                into[...] = summed
            held[p] = ([a for a in dims if a != axis], into)
    give = copy(0, final, last, twin)
    give.start()
    give.wait()
    keep = final.shape[0] // 2
    mine, other = final[...], last[...]
    out_ref[0] = jnp.where(core == 0, mine[:keep], other[keep:])
    out_ref[1] = jnp.where(core == 0, other[:keep], mine[keep:])


def reduce(total, scale, devices):
    _, vectors, width = total.shape
    rows = 2 * vectors // devices
    vm = pl.BlockSpec(memory_space=pltpu.VMEM)
    stages = []
    for _, lanes, _ in LANES:
        for stage in range(3):
            shape = (4,) * (2 - stage) + (rows, lanes * width // 4)
            stages += [pltpu.VMEM((3,) + shape, F32), pltpu.VMEM(shape, F32)]
    return pl.pallas_call(
        functools.partial(reduce_kernel, scale),
        out_shape=jax.ShapeDtypeStruct((2, rows // 2, width), F32),
        in_specs=[pl.BlockSpec(memory_space=pl.ANY)],
        out_specs=vm,
        scratch_shapes=[
            pltpu.VMEM((vectors, width), F32),
            pltpu.SemaphoreType.DMA,
            pltpu.VMEM((vectors, width), F32),
            pltpu.VMEM((4, 4, 4, rows, width), F32),
            pltpu.VMEM((rows, width), F32),
            pltpu.VMEM((rows, width), F32),
            *stages,
            pltpu.SemaphoreType.DMA((31,)),
            pltpu.SemaphoreType.DMA((31,)),
        ],
        compiler_params=pltpu.CompilerParams(
            collective_id=1, has_side_effects=True, vmem_limit_bytes=32 << 20
        ),
        name="reduce",
    )(pltpu.with_memory_space_constraint(total, pltpu.HBM))


def needs_of(source_blocks, tile_index, blocks, tiles_dir):
    me = lax.axis_index("rows")
    far_slot = jnp.maximum(source_blocks - blocks, 0)
    peer, copy = far_slot // 2, far_slot % 2
    differ = peer ^ me
    low = [(differ // STRIDE[axis]) % 2 for axis in range(3)]
    high = [(differ // (2 * STRIDE[axis])) % 2 for axis in range(3)]
    left_unit = high[0] + 2 * high[1] + 4 * high[2]
    right_unit = (low[0] ^ high[0]) + 2 * (low[1] ^ high[1]) + 4 * (low[2] ^ high[2])
    provider = (differ % 2) * 8 + right_unit
    block = jnp.arange(blocks, dtype=I32)[None, None, :]
    word = ((block * 16 + provider) * 2 + copy) * tiles_dir + jnp.maximum(tile_index, 0) + 1
    live = jnp.logical_and(tile_index >= 0, source_blocks >= blocks)
    unit = jnp.where(live, left_unit, -1)
    rows = jnp.stack([unit, word // 256, word % 256, jnp.zeros_like(word)])
    return rows.astype(F32).swapaxes(2, 3).reshape(8, -1)


def body(left, right, tiles, source_blocks, tile_index, send_blocks):
    block_rows = tiles.shape[-1]
    rows, _ = right.shape
    blocks = rows // block_rows
    devices = lax.axis_size("rows")
    scale = 1.0 / math.sqrt(rows * devices)
    source_blocks, tile_index = source_blocks.swapaxes(1, 2), tile_index.swapaxes(1, 2)
    info = needs_of(source_blocks, tile_index, blocks, tiles.shape[1])
    sent = send_blocks.T
    rights, lefts, needs, sents, total = gather(left, right, tiles, source_blocks, tile_index, info, sent)
    total = far(blocks, source_blocks.shape[1], rights, lefts, needs, sents, tiles, total)
    return reduce(total, scale, devices)


def solution(mesh):
    placed = (
        P("rows", None),
        P("rows", None),
        P(),
        P(None, "rows", None),
        P(None, "rows", None),
        P("rows", None),
    )
    return jax.shard_map(
        body, mesh=mesh, in_specs=placed, out_specs=P(None, "rows", None), check_vma=False
    )
```

```python
import functools
import math

import jax
import jax.numpy as jnp
from jax import lax
from jax.experimental import pallas as pl
from jax.experimental.pallas import tpu as pltpu
from jax.sharding import PartitionSpec as P

MESH = pl.DeviceIdType.MESH
BF16, F32, I32 = jnp.bfloat16, jnp.float32, jnp.int32

STRIDE = (2, 8, 32)


def coord(me, axis):
    return (me // STRIDE[axis]) % 4


def right_mate(me, axis):
    return me + STRIDE[axis] * (1 - 2 * (coord(me, axis) % 2))


def left_mate(me, axis):
    return me + STRIDE[axis] * (3 - 2 * coord(me, axis))


def other_core(me):
    return me + 1 - 2 * (me % 2)


def cut(rows, unit):
    third = rows // unit // 3
    sizes = [rows - 2 * third * unit, third * unit, third * unit]
    starts = [0, sizes[0], sizes[0] + sizes[1]]
    return list(zip(starts, sizes))


class Cube:
    def __init__(self, own, held, parts, mates, send, recv):
        self.own, self.held, self.parts, self.mates = own, held, parts, mates
        self.send, self.recv = send, recv

    def part(self, unit, p):
        start, size = self.parts[p]
        ref = self.own if unit == 0 else self.held.at[unit]
        return ref.at[pl.ds(start, size)]

    def hop(self, p, unit, axis):
        start, size = self.parts[p]
        into = unit + (1 << axis)
        at = p * 8 + into
        return pltpu.make_async_remote_copy(
            src_ref=self.part(unit, p),
            dst_ref=self.held.at[into].at[pl.ds(start, size)],
            send_sem=self.send.at[at],
            recv_sem=self.recv.at[at],
            device_id=(self.mates[axis],),
            device_id_type=MESH,
        )

    def order(self, p):
        return [(p + n) % 3 for n in range(3)]

    def phases(self):
        result = [[] for _ in range(7)]
        for p in range(len(self.parts)):
            a, b, c = self.order(p)
            ua, ub = 1 << a, 1 << b
            for n, (unit, axis) in enumerate(
                [(0, a), (0, b), (ua, b), (0, c), (ua, c), (ub, c), (ua + ub, c)]
            ):
                result[n].append((p, unit, axis))
        return result

    def start_own(self, axis_place):
        for p in range(len(self.parts)):
            self.hop(p, 0, self.order(p)[axis_place]).start()

    def forward(self, p, unit, axis):
        got = unit + (1 << axis)
        order = self.order(p)
        for later in order[order.index(axis) + 1 :]:
            self.hop(p, got, later).start()

    def drain(self):
        for phase in self.phases():
            for hop in phase:
                self.hop(*hop).wait_send()


def gather_kernel(
    blocks, slots,
    source_ref, tile_ref, left_ref, right_ref, block_ref, tiles_ref, info_ref, sent_ref,
    rights, lefts, needs, sents, total_ref,
    own_right, own_left, own_turned, tile_table, current, total, info, place_of, need_ref,
    local_sem, r_send, r_recv, l_send, l_recv, n_send, n_recv, s_send, s_recv, c_send, c_recv, d_send, d_recv,
):
    me = lax.axis_index("rows")
    right_mates = [right_mate(me, axis) for axis in range(3)]
    left_mates = [left_mate(me, axis) for axis in range(3)]
    twin = other_core(me)

    info_in = pltpu.make_async_copy(info_ref, info, local_sem.at[5])
    info_in.start()
    barrier = pltpu.get_barrier_semaphore()
    for mate in right_mates + left_mates + [twin]:
        pl.semaphore_signal(barrier, inc=1, device_id=(mate,), device_id_type=MESH)

    left_in = pltpu.make_async_copy(left_ref, own_left, local_sem.at[0])
    left_in.start()
    right_in = pltpu.make_async_copy(block_ref, own_right, local_sem.at[1])
    right_in.start()
    tiles_in = pltpu.make_async_copy(tiles_ref, tile_table.at[pl.ds(0, tiles_ref.shape[0])], local_sem.at[2])
    tiles_in.start()
    pl.semaphore_wait(barrier, 7)

    rows = right_ref.shape[0]
    turned_rows = own_turned.shape[0]
    right_cube = Cube(right_ref, rights.at[0], cut(rows, 16), right_mates, r_send, r_recv)
    left_cube = Cube(own_turned, lefts, cut(turned_rows, 16), left_mates, l_send, l_recv)
    need_cube = Cube(need_ref, needs, [(0, need_ref.shape[0])], left_mates, n_send, n_recv)
    sent_cube = Cube(sent_ref, sents.at[0], [(0, sent_ref.shape[0])], right_mates, s_send, s_recv)

    def across(p, unit):
        start, size = right_cube.parts[p]
        at = p * 8 + unit
        return pltpu.make_async_remote_copy(
            src_ref=right_cube.part(unit, p),
            dst_ref=rights.at[1].at[unit].at[pl.ds(start, size)],
            send_sem=c_send.at[at], recv_sem=c_recv.at[at], device_id=(twin,), device_id_type=MESH,
        )

    def across_sent(unit):
        return pltpu.make_async_remote_copy(
            src_ref=sent_cube.part(unit, 0), dst_ref=sents.at[1].at[unit],
            send_sem=d_send.at[unit], recv_sem=d_recv.at[unit], device_id=(twin,), device_id_type=MESH,
        )

    for place in range(3):
        right_cube.start_own(place)
    for place in range(3):
        sent_cube.start_own(place)
    across_sent(0).start()
    for p in range(3):
        across(p, 0).start()

    left_in.wait()
    block_rows = left_ref.shape[0] // blocks
    vectors = left_ref.shape[1]

    def turn(b, _):
        at = pl.multiple_of(b * block_rows, block_rows)
        to = pl.multiple_of(b * vectors, vectors)
        own_turned[pl.ds(to, vectors), :] = own_left[pl.ds(at, block_rows), :].T
        return 0

    lax.fori_loop(0, blocks, turn, 0)
    for place in range(3):
        left_cube.start_own(place)
    left_out = pltpu.make_async_copy(own_turned, lefts.at[0], local_sem.at[3])
    left_out.start()
    right_out = pltpu.make_async_copy(right_ref, rights.at[0].at[0], local_sem.at[4])
    right_out.start()
    sent_out = pltpu.make_async_copy(sent_ref, sents.at[0].at[0], local_sem.at[6])
    sent_out.start()

    info_in.wait()
    many = info.shape[1]
    down = lax.broadcasted_iota(I32, (many, many), 0)
    upto = jnp.where(down <= lax.broadcasted_iota(I32, (many, many), 1), 1.0, 0.0).astype(BF16)
    eight = lax.broadcasted_iota(I32, (8, many), 0)
    for d in range(2):
        mine = jnp.broadcast_to(info[d : d + 1, :], (8, many)) == eight.astype(F32)
        ranks = jnp.dot(jnp.where(mine, 1.0, 0.0).astype(BF16), upto, preferred_element_type=F32)
        place_of[...] = jnp.where(mine, ranks, 0.0)
        words = jnp.where(eight == 0, info[2 + d : 3 + d, :], jnp.where(eight == 1, info[4 + d : 5 + d, :], 0.0))
        words = words.astype(BF16)

        def list_for(unit, _):
            hit = place_of[pl.ds(unit, 1), :] == (down + 1).astype(F32)
            found = lax.dot_general(
                words, jnp.where(hit, 1.0, 0.0).astype(BF16), (((1,), (1,)), ((), ())), preferred_element_type=F32
            )
            word = (found[0:1] * 256.0 + found[1:2]).astype(I32)
            for line in range(many // 128):
                need_ref[unit, pl.ds(d * (many // 128) + line, 1), :] = word[:, line * 128 : line * 128 + 128]
            return 0

        lax.fori_loop(0, 8, list_for, 0)
    for place in range(3):
        need_cube.start_own(place)
    need_out = pltpu.make_async_copy(need_ref, needs.at[0], local_sem.at[5])
    need_out.start()

    tiles_in.wait()
    right_in.wait()
    zero_tile = tiles_ref.shape[0]
    tile_table[zero_tile] = jnp.zeros(tile_table.shape[1:], BF16)
    total[...] = jnp.zeros_like(total)
    group = 8
    groups = blocks // group

    def own_group(n, _):
        d = n // groups
        first = (n % groups) * group

        def row(e, _):
            b = first + e
            summed = jnp.zeros((block_rows, vectors), F32)
            for k0 in range(0, slots, 4):
                chosen, picked = [], []
                for k in range(k0, k0 + 4):
                    chosen.append(tile_table[tile_ref[d, k, b]])
                    picked.append(own_right[source_ref[d, k, b]])
                summed = summed + jnp.dot(
                    jnp.concatenate(chosen, axis=1), jnp.concatenate(picked, axis=0), preferred_element_type=F32
                )
            current[pl.ds(pl.multiple_of(e * block_rows, block_rows), block_rows), :] = summed.astype(BF16)
            return 0

        lax.fori_loop(0, group, row, 0)
        turned = jnp.concatenate(
            [own_turned[pl.ds(pl.multiple_of((first + e) * vectors, vectors), vectors), :] for e in range(group)], axis=1
        )
        total[d] = total[d] + jnp.dot(turned, current[...], preferred_element_type=F32)
        return 0

    def compute(lo, hi):
        lax.fori_loop(lo, hi, own_group, 0)

    plan = {0: (0, 3), 1: (3, 5), 2: (5, 8)}
    phases = list(zip(right_cube.phases(), left_cube.phases()))
    small = list(zip(need_cube.phases(), sent_cube.phases()))
    for n in range(7):
        if n in plan:
            compute(*plan[n])
        if n == 3:
            total_out = pltpu.make_async_copy(total, total_ref, local_sem.at[7])
            total_out.start()
        for hop in small[n][0]:
            need_cube.hop(*hop).wait_recv()
            need_cube.forward(*hop)
        for hop in small[n][1]:
            sent_cube.hop(*hop).wait_recv()
            sent_cube.forward(*hop)
            across_sent(hop[1] + (1 << hop[2])).start()
        for hop, lhop in zip(*phases[n]):
            right_cube.hop(*hop).wait_recv()
            right_cube.forward(*hop)
            across(hop[0], hop[1] + (1 << hop[2])).start()
            left_cube.hop(*lhop).wait_recv()
            left_cube.forward(*lhop)
    for cube in (right_cube, left_cube, need_cube, sent_cube):
        cube.drain()
    for unit in range(8):
        across_sent(unit).wait()
        for p in range(3):
            across(p, unit).wait()
    for copy in (left_out, right_out, need_out, sent_out, total_out):
        copy.wait()


def gather(left, right, tiles, source_blocks, tile_index, info, sent):
    rows, vectors = right.shape
    block_rows = tiles.shape[-1]
    blocks = rows // block_rows
    table = tiles.reshape(-1, block_rows, block_rows)
    offset = jnp.arange(2, dtype=I32)[:, None, None] * tiles.shape[1]
    own = jnp.logical_and(tile_index >= 0, source_blocks < blocks)
    tile_index = jnp.where(own, tile_index + offset, table.shape[0])
    source_blocks = jnp.where(own, source_blocks, 0)
    any_spec = pl.BlockSpec(memory_space=pl.ANY)
    smem = pl.BlockSpec(memory_space=pltpu.SMEM)
    dma = pltpu.SemaphoreType.DMA
    return pl.pallas_call(
        functools.partial(gather_kernel, blocks, source_blocks.shape[1]),
        out_shape=(
            jax.ShapeDtypeStruct((2, 8, rows, vectors), BF16),
            pltpu.VMEM((8, blocks * vectors, block_rows), BF16),
            jax.ShapeDtypeStruct((8, 8) + (2 * info.shape[1] // 128, 128), I32),
            jax.ShapeDtypeStruct((2, 8) + sent.shape, I32),
            jax.ShapeDtypeStruct((2, vectors, vectors), F32),
        ),
        in_specs=[smem, smem] + [any_spec] * 6,
        out_specs=(any_spec, pl.BlockSpec(memory_space=pltpu.VMEM)) + (any_spec,) * 3,
        scratch_shapes=[
            pltpu.VMEM((blocks, block_rows, vectors), BF16),
            pltpu.VMEM((rows, vectors), BF16),
            pltpu.VMEM((blocks * vectors, block_rows), BF16),
            pltpu.VMEM((table.shape[0] + 1, block_rows, block_rows), BF16),
            pltpu.VMEM((8 * block_rows, vectors), BF16),
            pltpu.VMEM((2, vectors, vectors), F32),
            pltpu.VMEM(info.shape, F32),
            pltpu.VMEM(info.shape, F32),
            pltpu.VMEM((8, 2 * info.shape[1] // 128, 128), I32),
            dma((8,)),
            dma((24,)), dma((24,)), dma((24,)), dma((24,)),
            dma((8,)), dma((8,)), dma((8,)), dma((8,)),
            dma((24,)), dma((24,)), dma((8,)), dma((8,)),
        ],
        compiler_params=pltpu.CompilerParams(
            collective_id=0, has_side_effects=True, vmem_limit_bytes=28 << 20
        ),
        name="gather",
    )(source_blocks, tile_index, left, right, right.reshape(blocks, block_rows, vectors), table, info, sent)


GROUP = 16
DEPTH = 4


def far_kernel(
    blocks, many, tiles_dir,
    rights, lefts, needs, sents, tiles_ref, total_in, total_ref,
    need_s, sent_s, terms, order, tile_table, right_buf, current, total, sem, rsem,
):
    me = lax.axis_index("rows")
    block_rows, vectors = right_buf.shape[-2] // GROUP, right_buf.shape[-1]
    copies = [pltpu.make_async_copy(tiles_ref, tile_table.at[pl.ds(0, tiles_ref.shape[0])], sem.at[0])]
    copies.append(pltpu.make_async_copy(total_in, total, sem.at[1]))
    for j in range(8):
        copies.append(pltpu.make_async_copy(needs.at[j, j], need_s.at[j], sem.at[2 + j]))
    copies.append(pltpu.make_async_copy(sents, sent_s, sem.at[10]))
    for copy in copies[2:] + copies[:2]:
        copy.start()
    for copy in copies[2:]:
        copy.wait()

    zero_tile = 2 * tiles_dir
    tile_bits = (tiles_dir - 1).bit_length()
    block_bits = (blocks - 1).bit_length()
    ADDR, ROW = 8, 8 + 4 + block_bits
    UNROLL = 8

    most = 8 * many
    single_most = 8 * blocks + 3 * GROUP
    pair_at = [d * (most + 2 * GROUP) for d in range(2)]
    single_at = [2 * (most + 2 * GROUP) + d * single_most for d in range(2)]

    def list_dir(d):
        def unit(j, state):
            z, x, y = coord(me, 0), coord(me, 1), coord(me, 2)
            z = jnp.where(j & 1 == 1, 3 - z, z)
            x = jnp.where(j & 2 == 2, 3 - x, x)
            y = jnp.where(j & 4 == 4, 3 - y, y)
            holder = y * STRIDE[2] + x * STRIDE[1] + z * STRIDE[0] + me % 2
            base = d * (many // 128)

            def word(k):
                return need_s[j, base + (k >> 7), k & 127]

            def more(state):
                k, pair, single, last, first = state
                for u in range(UNROLL):
                    w = word(k + u)
                    live = jnp.minimum(w, 1)
                    v = jnp.maximum(w - 1, 0)
                    slot = (v >> tile_bits) & 31
                    block = jnp.maximum(sent_s[slot >> 4, (slot >> 1) & 7, slot & 1, holder], 0)
                    b = v >> (tile_bits + 5)
                    address = ((slot >> 1) << block_bits) + block
                    term = (((j << block_bits) + b) << ROW) + (address << ADDR) + d * tiles_dir + (v & (tiles_dir - 1))
                    second = jnp.where(b == last, live, 0)
                    terms[single] = term
                    terms[pair] = first
                    terms[pair + 1] = term
                    pair = pair + 2 * second
                    single = single + live - 2 * second
                    first = term
                    last = jnp.where(second == 1, -1, b)
                return k + UNROLL, pair, single, last, first

            def going(state):
                k = state[0]
                return jnp.logical_and(k < many, word(jnp.minimum(k, many - 1)) > 0)

            return lax.while_loop(going, more, (jnp.int32(0), *state, jnp.int32(-1), jnp.int32(0)))[1:3]

        ends = lax.fori_loop(0, 8, unit, (jnp.int32(pair_at[d]), jnp.int32(single_at[d])))
        counts = []
        for end, first in zip(ends, (pair_at[d], single_at[d])):
            for u in range(GROUP):
                terms[end + u] = zero_tile
            counts.append((end - first + GROUP - 1) // GROUP)
        return counts

    def start(g):
        at = order[g] >> 2
        slot = g % DEPTH
        for e in range(GROUP):
            address = (terms[at + e] >> ADDR) & ((16 << block_bits) - 1)
            provider, block = address >> block_bits, address & (blocks - 1)
            pltpu.make_async_copy(
                rights.at[provider >> 3, provider & 7, pl.ds(pl.multiple_of(block * block_rows, block_rows), block_rows)],
                right_buf.at[slot, pl.ds(e * block_rows, block_rows)],
                rsem.at[slot],
            ).start()

    count = jnp.int32(0)
    for d in range(2):
        begun = count
        for kind, (many_groups, first) in enumerate(zip(list_dir(d), (pair_at[d], single_at[d]))):

            def note(n, _, kind=kind, first=first, d=d, count=count):
                order[count + n] = ((first + n * GROUP) << 2) + d * 2 + kind
                return 0

            lax.fori_loop(0, many_groups, note, 0)
            count = count + many_groups
        for g in range(DEPTH - 1):

            @pl.when(jnp.logical_and(g >= begun, g < count))
            def _(g=g):
                start(g)

    for copy in copies[:2]:
        copy.wait()
    tile_table[zero_tile] = jnp.zeros(tile_table.shape[1:], BF16)

    def left_of(term):
        row = term >> ROW
        return lefts[row >> block_bits, pl.ds(pl.multiple_of((row & (blocks - 1)) * vectors, vectors), vectors), :]

    def step(g, _):
        @pl.when(g + DEPTH - 1 < count)
        def _():
            start(g + DEPTH - 1)

        word = order[g]
        at, d = word >> 2, (word >> 1) & 1
        slot = g % DEPTH
        pltpu.make_async_copy(right_buf.at[slot], right_buf.at[slot], rsem.at[slot]).wait()
        for kind, width in ((0, 2), (1, 1)):

            @pl.when(word & 1 == kind)
            def _(width=width):
                turned = []
                for n, e in enumerate(range(0, GROUP, width)):
                    chosen = [tile_table[terms[at + e + u] & 255] for u in range(width)]
                    current[pl.ds(n * block_rows, block_rows), :] = jnp.dot(
                        jnp.concatenate(chosen, axis=1) if width > 1 else chosen[0],
                        right_buf[slot, pl.ds(e * block_rows, width * block_rows), :],
                        preferred_element_type=F32,
                    ).astype(BF16)
                    turned.append(left_of(terms[at + e]))
                total[d] = total[d] + jnp.dot(
                    jnp.concatenate(turned, axis=1),
                    current[pl.ds(0, len(turned) * block_rows), :],
                    preferred_element_type=F32,
                )

        return 0

    lax.fori_loop(0, count, step, 0)
    out = pltpu.make_async_copy(total, total_ref, sem.at[0])
    out.start()
    out.wait()


def far(blocks, slots, rights, lefts, needs, sents, tiles, total):
    rows, vectors = rights.shape[2:]
    block_rows = tiles.shape[-1]
    tiles_dir = tiles.shape[1]
    table = tiles.reshape(-1, block_rows, block_rows)
    any_spec = pl.BlockSpec(memory_space=pl.ANY)
    dma = pltpu.SemaphoreType.DMA
    return pl.pallas_call(
        functools.partial(far_kernel, blocks, blocks * slots, tiles_dir),
        out_shape=jax.ShapeDtypeStruct(total.shape, F32),
        in_specs=[any_spec, pl.BlockSpec(memory_space=pltpu.VMEM)] + [any_spec] * 4,
        out_specs=any_spec,
        scratch_shapes=[
            pltpu.SMEM((8,) + needs.shape[2:], I32),
            pltpu.SMEM(sents.shape, I32),
            pltpu.SMEM((2 * (8 * blocks * slots + 2 * GROUP + 8 * blocks + 3 * GROUP),), I32),
            pltpu.SMEM((2 * (8 * blocks * slots + 8 * blocks) // GROUP + 8,), I32),
            pltpu.VMEM((table.shape[0] + 1, block_rows, block_rows), BF16),
            pltpu.VMEM((DEPTH, GROUP * block_rows, vectors), BF16),
            pltpu.VMEM((GROUP * block_rows, vectors), BF16),
            pltpu.VMEM(total.shape, F32),
            dma((26,)), dma((DEPTH,)),
        ],
        compiler_params=pltpu.CompilerParams(vmem_limit_bytes=28 << 20),
        name="far",
    )(rights, pltpu.with_memory_space_constraint(lefts, pltpu.VMEM), needs, sents, table, total)


LANES = ((2, 2, (2, 1, 0)), (0, 1, (1, 0, 2)), (1, 1, (0, 2, 1)))


def reduce_kernel(scale, total_ref, out_ref, mine_core, local_sem, got_core, half, final, last, *rest):
    stages, (send, recv) = rest[:-2], rest[-2:]
    me = lax.axis_index("rows")
    core = me % 2
    twin = other_core(me)

    def at(axis, n):
        c = coord(me, axis)
        return me + STRIDE[axis] * ((c + n) % 4 - c)

    mine_in = pltpu.make_async_copy(total_ref.at[core], mine_core, local_sem)
    mine_in.start()
    peers = [twin] + [at(axis, n) for axis in range(3) for n in range(1, 4)]
    barrier = pltpu.get_barrier_semaphore()
    for peer in peers:
        pl.semaphore_signal(barrier, inc=1, device_id=(peer,), device_id_type=MESH)
    pl.semaphore_wait(barrier, len(peers))

    def copy(n, src, dst, peer):
        return pltpu.make_async_remote_copy(
            src_ref=src, dst_ref=dst, send_sem=send.at[n], recv_sem=recv.at[n], device_id=(peer,), device_id_type=MESH
        )

    unit = got_core.shape[-1] // 4
    swaps = []
    for p, (first, lanes, order) in enumerate(LANES):
        columns = pl.ds(first * unit, lanes * unit)
        swaps.append(
            copy(28 + p, total_ref.at[1 - core].at[:, columns], got_core.at[:, columns], twin)
        )
        swaps[-1].start()
    mine_in.wait()

    everything = slice(None)
    held = []
    for first, lanes, order in LANES:
        held.append(([2, 1, 0], half.at[:, :, :, :, pl.ds(first * unit, lanes * unit)]))
    for stage in range(3):
        started = []
        for p, (first, lanes, order) in enumerate(LANES):
            dims, ref = held[p]
            axis = order[stage]
            skip = (everything,) * dims.index(axis)
            got = stages[2 * (3 * p + stage)]
            if stage == 0:
                swaps[p].wait()
                columns = slice(first * unit, (first + lanes) * unit)
                both = (mine_core[:, columns] + got_core[:, columns]) * scale
                half[:, :, :, :, columns] = both.reshape(half.shape[:-1] + (lanes * unit,))
            for n in (2, 1, 3):
                theirs = (coord(me, axis) + n) % 4
                sending = copy(1 + 9 * p + 3 * stage + n - 1, ref.at[skip + (theirs,)], got.at[n - 1], at(axis, n))
                sending.start()
                started.append((p, sending))
        for p, (first, lanes, order) in enumerate(LANES):
            dims, ref = held[p]
            axis = order[stage]
            skip = (everything,) * dims.index(axis)
            got, into = stages[2 * (3 * p + stage)], stages[2 * (3 * p + stage) + 1]
            for q, sending in started:
                if q == p:
                    sending.wait()
            summed = ref[skip + (coord(me, axis),)] + got[0] + got[1] + got[2]
            if stage == 2:
                final[:, first * unit : (first + lanes) * unit] = summed
            else:
                into[...] = summed
            held[p] = ([a for a in dims if a != axis], into)
    give = copy(0, final, last, twin)
    give.start()
    give.wait()
    keep = final.shape[0] // 2
    mine, other = final[...], last[...]
    out_ref[0] = jnp.where(core == 0, mine[:keep], other[keep:])
    out_ref[1] = jnp.where(core == 0, other[:keep], mine[keep:])


def reduce(total, scale, devices):
    _, vectors, width = total.shape
    rows = 2 * vectors // devices
    vm = pl.BlockSpec(memory_space=pltpu.VMEM)
    stages = []
    for _, lanes, _ in LANES:
        for stage in range(3):
            shape = (4,) * (2 - stage) + (rows, lanes * width // 4)
            stages += [pltpu.VMEM((3,) + shape, F32), pltpu.VMEM(shape, F32)]
    return pl.pallas_call(
        functools.partial(reduce_kernel, scale),
        out_shape=jax.ShapeDtypeStruct((2, rows // 2, width), F32),
        in_specs=[pl.BlockSpec(memory_space=pl.ANY)],
        out_specs=vm,
        scratch_shapes=[
            pltpu.VMEM((vectors, width), F32),
            pltpu.SemaphoreType.DMA,
            pltpu.VMEM((vectors, width), F32),
            pltpu.VMEM((4, 4, 4, rows, width), F32),
            pltpu.VMEM((rows, width), F32),
            pltpu.VMEM((rows, width), F32),
            *stages,
            pltpu.SemaphoreType.DMA((31,)),
            pltpu.SemaphoreType.DMA((31,)),
        ],
        compiler_params=pltpu.CompilerParams(
            collective_id=1, has_side_effects=True, vmem_limit_bytes=32 << 20
        ),
        name="reduce",
    )(pltpu.with_memory_space_constraint(total, pltpu.HBM))


def needs_of(source_blocks, tile_index, blocks, tiles_dir):
    me = lax.axis_index("rows")
    far_slot = jnp.maximum(source_blocks - blocks, 0)
    peer, copy = far_slot // 2, far_slot % 2
    differ = peer ^ me
    low = [(differ // STRIDE[axis]) % 2 for axis in range(3)]
    high = [(differ // (2 * STRIDE[axis])) % 2 for axis in range(3)]
    left_unit = high[0] + 2 * high[1] + 4 * high[2]
    right_unit = (low[0] ^ high[0]) + 2 * (low[1] ^ high[1]) + 4 * (low[2] ^ high[2])
    provider = (differ % 2) * 8 + right_unit
    block = jnp.arange(blocks, dtype=I32)[None, None, :]
    word = ((block * 16 + provider) * 2 + copy) * tiles_dir + jnp.maximum(tile_index, 0) + 1
    live = jnp.logical_and(tile_index >= 0, source_blocks >= blocks)
    unit = jnp.where(live, left_unit, -1)
    rows = jnp.stack([unit, word // 256, word % 256, jnp.zeros_like(word)])
    return rows.astype(F32).swapaxes(2, 3).reshape(8, -1)


def body(left, right, tiles, source_blocks, tile_index, send_blocks):
    block_rows = tiles.shape[-1]
    rows, _ = right.shape
    blocks = rows // block_rows
    devices = lax.axis_size("rows")
    scale = 1.0 / math.sqrt(rows * devices)
    source_blocks, tile_index = source_blocks.swapaxes(1, 2), tile_index.swapaxes(1, 2)
    info = needs_of(source_blocks, tile_index, blocks, tiles.shape[1])
    sent = send_blocks.T
    rights, lefts, needs, sents, total = gather(left, right, tiles, source_blocks, tile_index, info, sent)
    total = far(blocks, source_blocks.shape[1], rights, lefts, needs, sents, tiles, total)
    return reduce(total, scale, devices)


def solution(mesh):
    placed = (
        P("rows", None),
        P("rows", None),
        P(),
        P(None, "rows", None),
        P(None, "rows", None),
        P("rows", None),
    )
    return jax.shard_map(
        body, mesh=mesh, in_specs=placed, out_specs=P(None, "rows", None), check_vma=False
    )
```
